512 devices in a mesh: space: 32 (over y, z_hi), filt: 16 (over z_lo, x, core).
Axes of the slice: x: 4, y: 8, z: 8 (z_hi: 4, z_lo: 2; z = z_hi * 2 + z_lo), core: 2. Of those that a mesh axis runs over, the one named last changes fastest.
Arguments:
- activations: bfloat16 [64, 32, 128, 128], P('space', None, 'filt'), may hold values from -6 to 6
- weight: bfloat16 [3, 3, 3, 128, 128], P(None, None, None, None, 'filt'), may hold values from -0.109375 to 0.109375
- grad_out: bfloat16 [64, 32, 128, 128], P('space', None, 'filt'), may hold values from -6 to 6
Outputs:
- output: float32 [64, 32, 128, 128], P('space', None, 'filt')
- grad_in: float32 [64, 32, 128, 128], P('space', None, 'filt')
- weight_grad: float32 [3, 3, 3, 128, 128], P(None, None, None, None, 'filt')
The draws below stay inside these ranges and needn't reach their ends.
All inputs are finite; a program needn't handle non-finite values.
Results may differ from the reference program's by a relative error of at most 0.0003.
Values may be sent and summed in bfloat16 or wider, within the bound.
No kernel may reach another device: no remote copies, remote signals or barrier semaphores. Data moves between devices by JAX's collectives and lax.ppermute only.
A program may use at most 64 MiB of HBM per device.

```python
import jax
import jax.numpy as jnp
from jax import lax

C = 128
H = 32
W = 128
NZ = 64


def steps_of(key, extent, cuts, low, high):
    loudness = 1.0
    for dim, parts in cuts:
        heights = jax.random.uniform(jax.random.fold_in(jax.random.fold_in(key, 6), dim), (parts,), jnp.float32, low / len(cuts), high / len(cuts))
        loudness = loudness * jnp.repeat(jnp.exp(heights), extent[dim] // parts).reshape((-1,) + (1,) * (len(extent) - 1 - dim))
    return loudness


def scatter_about(rng, extent, width, bound, split=(), kind=jnp.bfloat16):
    values = width * jax.random.normal(rng, extent, jnp.float32)
    if split:
        values = values * steps_of(rng, extent, split, -0.22, 0.18)
    return jnp.clip(values, -bound, bound).astype(kind)


def setup_inputs(seed: int = 0) -> dict:
    splits = jax.random.split(jax.random.key(seed), 4)
    activations = scatter_about(splits[0], (NZ, H, C, W), 1.0, 6.0, ((0, 32), (2, 16)))
    weight = scatter_about(splits[1], (3, 3, 3, C, C), (27 * C) ** -0.5, 0.109375, ((4, 16),))
    grad_out = scatter_about(splits[2], (NZ, H, C, W), 1.0, 6.0, ((0, 32), (2, 16)))
    return dict(activations=activations, weight=weight, grad_out=grad_out)


def convolve(volume, kernel):
    return lax.conv_general_dilated(volume[None], kernel, (1, 1, 1), "SAME", dimension_numbers=("NDHWC", "DHWIO", "NDHWC"), precision=lax.Precision.HIGHEST)[0]


def reference(activations, weight, grad_out):
    inputs = activations.astype(jnp.float32).transpose(0, 1, 3, 2)
    kernel = weight.astype(jnp.float32)
    cotangent = grad_out.astype(jnp.float32).transpose(0, 1, 3, 2)
    output = convolve(inputs, kernel).transpose(0, 1, 3, 2)
    flipped = jnp.flip(kernel, (0, 1, 2)).transpose(0, 1, 2, 4, 3)
    grad_in = convolve(cotangent, flipped).transpose(0, 1, 3, 2)
    padded = jnp.pad(inputs, ((1, 1), (1, 1), (1, 1), (0, 0)))
    blocks = []
    for shift_a in range(3):
        for shift_b in range(3):
            for shift_c in range(3):
                window = padded[shift_a:shift_a + NZ, shift_b:shift_b + H, shift_c:shift_c + W]
                blocks.append(jnp.einsum("zhwi,zhwo->io", window, cotangent, precision=lax.Precision.HIGHEST))
    norm_factor = float(NZ * H * W) ** -0.5
    weight_grad = jnp.stack(blocks, 0).reshape(3, 3, 3, C, C) * norm_factor
    return (output, grad_in, weight_grad)
```

```python
import functools

import jax
import jax.numpy as jnp
from jax import lax
from jax.experimental import pallas as pl
from jax.experimental.pallas import tpu as pltpu
from jax.sharding import Mesh
from jax.sharding import PartitionSpec as P

SPACE = ("y", "zh")
FILT = ("zl", "x", "core")
CHIPS = ("zl", "x")
BF, F32 = jnp.bfloat16, jnp.float32


def vmem_specs(n):
    return [pl.BlockSpec(memory_space=pltpu.VMEM)] * n


def call(kernel, outs, ins, scratch=(), smem=0, flops=0, name=None):
    specs = [pl.BlockSpec(memory_space=pltpu.SMEM)] * smem + vmem_specs(len(ins) - smem)
    moved = sum(a.size * a.dtype.itemsize for a in ins) + sum(o.size * o.dtype.itemsize for o in outs)
    return pl.pallas_call(
        kernel,
        out_shape=tuple(outs),
        in_specs=specs,
        out_specs=tuple(vmem_specs(len(outs))),
        scratch_shapes=list(scratch),
        cost_estimate=pl.CostEstimate(flops=flops, transcendentals=0, bytes_accessed=moved),
        name=name,
    )(*ins)


def pack_kernel(x_ref, g_ref, o_ref):
    n, _, nz, nr = o_ref.shape[:4]
    step = nr - 2
    rows = x_ref.shape[1]
    zero = jnp.zeros(x_ref.shape[2:], x_ref.dtype)
    for k, ref in enumerate((x_ref, g_ref)):
        for z in range(nz):
            for d in range(n):
                for r in range(nr):
                    h = d * step + r - 1
                    o_ref[d, k, z, r] = ref[z, h] if 0 <= h < rows else zero


def shifted(value):
    lane = lax.broadcasted_iota(jnp.int32, value.shape, 1)
    w = value.shape[1]
    left = jnp.where(lane == 0, 0.0, pltpu.roll(value, 1, 1))
    right = jnp.where(lane == w - 1, 0.0, pltpu.roll(value, w - 1, 1))
    return left.astype(BF), value.astype(BF), right.astype(BF)


def block_of(plane_ref, k, r, z=None):
    n = plane_ref.shape[0]
    if z is None:
        parts = [plane_ref[d, k, r].astype(F32) for d in range(n)]
    else:
        parts = [plane_ref[d, k, z, r].astype(F32) for d in range(n)]
    return jnp.concatenate(parts, 0)


def planes(own_ref, before_ref, after_ref):
    yield before_ref, None
    yield own_ref, 0
    yield own_ref, 1
    yield after_ref, None


def build(own_ref, before_ref, after_ref, k, s_ref):
    nr = own_ref.shape[3]
    nh = nr - 2
    ch = own_ref.shape[0] * own_ref.shape[4]
    w = own_ref.shape[5]
    for p, (ref, z) in enumerate(planes(own_ref, before_ref, after_ref)):
        for r in range(nr):
            for c, v in enumerate(shifted(block_of(ref, k, r, z))):
                for h in range(nh):
                    b = r - h
                    if 0 <= b < 3:
                        s_ref[p, pl.ds((3 * b + c) * ch, ch), pl.ds(h * w, w)] = v


def wgrad_kernel(core_ref, own_ref, before_ref, after_ref, o_ref, s_ref, g_ref):
    n, _, nz, nr, cg, w = own_ref.shape
    nh = nr - 2
    ch = n * cg
    build(own_ref, before_ref, after_ref, 0, s_ref)
    for z in range(nz):
        for h in range(nh):
            g_ref[z, :, pl.ds(h * w, w)] = block_of(own_ref, 1, h + 1, z).astype(BF)
    core = core_ref[0]
    for a in range(3):
        for b in range(3):
            total = None
            for z in range(nz):
                part = lax.dot_general(
                    g_ref[z],
                    s_ref[z + a, pl.ds(3 * b * ch, 3 * ch), :],
                    (((1,), (1,)), ((), ())),
                    preferred_element_type=F32,
                )
                total = part if total is None else total + part
            for c in range(3):
                for d in range(n):
                    slot = (d % 2) ^ core
                    o_ref[slot, d // 2, 9 * a + 3 * b + c] = total[d * cg : (d + 1) * cg, c * ch : (c + 1) * ch]


def weights_kernel(core_ref, mine_ref, other_ref, wt_ref, wf_ref):
    m, taps, cg, ch = mine_ref.shape
    first = core_ref[0] == 0
    for t in range(taps):
        a, bc = t // 9, t % 9
        parts = []
        for q in range(m):
            mine, other = mine_ref[q, t].astype(F32), other_ref[q, t].astype(F32)
            parts += [jnp.where(first, mine, other), jnp.where(first, other, mine)]
        block = jnp.concatenate(parts, 0)
        wt_ref[a, :, pl.ds(bc * ch, ch)] = block.astype(BF)
        wf_ref[2 - a, :, pl.ds((8 - bc) * ch, ch)] = block.T.astype(BF)


def conv_kernel(own_ref, before_ref, after_ref, wt_ref, wf_ref, o_ref, s_ref):
    n, _, nz, nr, cg, w = own_ref.shape
    nh = nr - 2
    for k, w_ref in enumerate((wt_ref, wf_ref)):
        build(own_ref, before_ref, after_ref, k, s_ref.at[k])
        for z in range(nz):
            total = None
            for a in range(3):
                part = jnp.dot(w_ref[a], s_ref[k, z + a], preferred_element_type=F32)
                total = part if total is None else total + part
            for d in range(n):
                for h in range(nh):
                    o_ref[d, k, z, h] = total[d * cg : (d + 1) * cg, h * w : (h + 1) * w]


def body(activations, weight, grad_out):
    nz, rows, cg, w = activations.shape
    n = lax.axis_size(FILT)
    chips = lax.axis_size(CHIPS)
    ns = lax.axis_size(SPACE)
    ch = n * cg
    nr = rows // n + 2
    nh = nr - 2
    norm = float(nz * ns * rows * w) ** (-0.5)
    core = lax.axis_index("core").astype(jnp.int32).reshape(1)
    up = [(i, i + 1) for i in range(ns - 1)]
    down = [(j, i) for i, j in up]
    swap = [(0, 1), (1, 0)]
    sds = jax.ShapeDtypeStruct

    (packed,) = call(pack_kernel, [sds((n, 2, nz, nr, cg, w), BF)], [activations, grad_out], name="pack")
    own = lax.all_to_all(packed, FILT, 0, 0, tiled=True)

    flat_w = weight.transpose(0, 1, 2, 4, 3).reshape(27, cg, ch)
    spread = jnp.broadcast_to(flat_w[None], (chips, 27, cg, ch))
    mine = lax.all_to_all(spread, CHIPS, 0, 0, tiled=True)
    other = lax.ppermute(mine, "core", swap)
    wt, wf = call(
        weights_kernel, [sds((3, ch, 9 * ch), BF)] * 2, [core, mine, other], smem=1, name="weights"
    )

    before = lax.ppermute(own[:, :, nz - 1], SPACE, up)
    after = lax.ppermute(own[:, :, 0], SPACE, down)

    (partial,) = call(
        wgrad_kernel,
        [sds((2, chips, 27, cg, ch), F32)],
        [core, own, before, after],
        scratch=[pltpu.VMEM((nz + 2, 9 * ch, nh * w), BF), pltpu.VMEM((nz, ch, nh * w), BF)],
        smem=1,
        flops=2 * 27 * ch * ch * nz * nh * w,
        name="wgrad",
    )
    pair = partial[0] + lax.ppermute(partial[1], "core", swap)
    pieces = lax.all_to_all(pair, CHIPS, 0, 0, tiled=True).reshape(chips, 27, cg, ch)
    group = pieces.sum(0)

    (blocks,) = call(
        conv_kernel,
        [sds((n, 2, nz, nh, cg, w), F32)],
        [own, before, after, wt, wf],
        scratch=[pltpu.VMEM((2, nz + 2, 9 * ch, nh * w), BF)],
        flops=2 * 2 * 27 * ch * ch * nz * nh * w,
        name="conv",
    )
    back = lax.all_to_all(blocks, FILT, 0, 0, tiled=True)
    back = back.transpose(1, 2, 0, 3, 4, 5).reshape(2, nz, rows, cg, w)

    padded = jnp.pad(group, ((0, ns - 27), (0, 0), (0, 0)))
    shares = lax.all_to_all(padded, SPACE, 0, 0, tiled=True)
    tap = shares.sum(0) * norm
    taps = lax.all_to_all(jnp.broadcast_to(tap[None], (ns, cg, ch)), SPACE, 0, 0, tiled=True)
    weight_grad = taps[:27].reshape(3, 3, 3, cg, ch).transpose(0, 1, 2, 4, 3)
    return back[0], back[1], weight_grad


def solution(mesh):
    fine = Mesh(mesh.devices.reshape(8, 4, 2, 4, 2), SPACE + FILT)
    return jax.shard_map(
        body,
        mesh=fine,
        in_specs=(
            P(SPACE, None, FILT, None),
            P(None, None, None, None, FILT),
            P(SPACE, None, FILT, None),
        ),
        out_specs=(
            P(SPACE, None, FILT, None),
            P(SPACE, None, FILT, None),
            P(None, None, None, None, FILT),
        ),
        check_vma=False,
    )
```

```python
import jax
import jax.numpy as jnp
from jax import lax
from jax.experimental import pallas as pl
from jax.experimental.pallas import tpu as pltpu
from jax.sharding import Mesh
from jax.sharding import PartitionSpec as P


SPACE = ("y", "zh")
FILT = ("zl", "x", "core")
CHIPS = ("zl", "x")
BF, F32 = jnp.bfloat16, jnp.float32


def vmem_specs(n):
    return [pl.BlockSpec(memory_space=pltpu.VMEM)] * n


def call(kernel, outs, ins, scratch=(), smem=0, flops=0):
    specs = [pl.BlockSpec(memory_space=pltpu.SMEM)] * smem + vmem_specs(len(ins) - smem)
    moved = sum(a.size * a.dtype.itemsize for a in ins) + sum(o.size * o.dtype.itemsize for o in outs)
    return pl.pallas_call(
        kernel,
        out_shape=tuple(outs),
        in_specs=specs,
        out_specs=tuple(vmem_specs(len(outs))),
        scratch_shapes=list(scratch),
        cost_estimate=pl.CostEstimate(flops=flops, transcendentals=0, bytes_accessed=moved),
    )(*ins)


def pack_kernel(x_ref, o_ref):
    n, nz, nr = o_ref.shape[:3]
    rows = x_ref.shape[1]
    zero = jnp.zeros(x_ref.shape[2:], x_ref.dtype)
    for z in range(nz):
        for d in range(n):
            for r in range(nr):
                h = d * (nr - 2) + r - 1
                o_ref[d, z, r] = x_ref[z, h] if 0 <= h < rows else zero


def shifted(value):
    lane = lax.broadcasted_iota(jnp.int32, value.shape, 1)
    w = value.shape[1]
    left = jnp.where(lane == 0, 0.0, pltpu.roll(value, 1, 1))
    right = jnp.where(lane == w - 1, 0.0, pltpu.roll(value, w - 1, 1))
    return left.astype(BF), value.astype(BF), right.astype(BF)


def block_of(ref, r, z=None):
    n = ref.shape[0]
    parts = [(ref[d, r] if z is None else ref[d, z, r]).astype(F32) for d in range(n)]
    return jnp.concatenate(parts, 0)


def build(own_ref, before_ref, after_ref, s_ref):
    n, nz, nr, cg, w = own_ref.shape
    nh, ch = nr - 2, n * cg
    planes = [(before_ref, None)] + [(own_ref, z) for z in range(nz)] + [(after_ref, None)]
    for p, (ref, z) in enumerate(planes):
        for r in range(nr):
            for c, v in enumerate(shifted(block_of(ref, r, z))):
                for h in range(nh):
                    b = r - h
                    if 0 <= b < 3:
                        s_ref[p, pl.ds((3 * b + c) * ch, ch), pl.ds(h * w, w)] = v


def wgrad_kernel(core_ref, x_ref, before_ref, after_ref, g_ref, keep_ref, send_ref, s_ref, t_ref, o_ref, sems):
    n, nz, nr, cg, w = x_ref.shape
    nh, ch = nr - 2, n * cg
    build(x_ref, before_ref, after_ref, s_ref)
    for z in range(nz):
        for h in range(nh):
            t_ref[z, :, pl.ds(h * w, w)] = block_of(g_ref, h + 1, z).astype(BF)
    core = core_ref[0]
    for a in range(3):
        for b in range(3):
            total = None
            for z in range(nz):
                part = lax.dot_general(
                    t_ref[z],
                    s_ref[z + a, pl.ds(3 * b * ch, 3 * ch), :],
                    (((1,), (1,)), ((), ())),
                    preferred_element_type=F32,
                )
                total = part if total is None else total + part
            for c in range(3):
                for d in range(n):
                    slot = (d % 2) ^ core
                    o_ref[slot, d // 2, 9 * a + 3 * b + c] = total[d * cg : (d + 1) * cg, c * ch : (c + 1) * ch]
    copies = [
        pltpu.make_async_copy(o_ref.at[1], send_ref, sems.at[1]),
        pltpu.make_async_copy(o_ref.at[0], keep_ref, sems.at[0]),
    ]
    for copy in copies:
        copy.start()
    for copy in copies:
        copy.wait()


def weights_kernel(core_ref, mine_ref, other_ref, wt_ref, wf_ref):
    m, taps, _, ch = mine_ref.shape
    first = core_ref[0] == 0
    for t in range(taps):
        a, bc = t // 9, t % 9
        parts = []
        for q in range(m):
            mine, other = mine_ref[q, t].astype(F32), other_ref[q, t].astype(F32)
            parts += [jnp.where(first, mine, other), jnp.where(first, other, mine)]
        block = jnp.concatenate(parts, 0)
        wt_ref[a, :, pl.ds(bc * ch, ch)] = block.astype(BF)
        wf_ref[2 - a, :, pl.ds((8 - bc) * ch, ch)] = block.T.astype(BF)


def conv_kernel(x_ref, xb_ref, xa_ref, g_ref, gb_ref, ga_ref, wt_ref, wf_ref, o_ref, s_ref):
    n, nz, nr, cg, w = x_ref.shape
    nh = nr - 2
    for k, (refs, w_ref) in enumerate((((x_ref, xb_ref, xa_ref), wt_ref), ((g_ref, gb_ref, ga_ref), wf_ref))):
        build(*refs, s_ref.at[k])
        for z in range(nz):
            total = None
            for a in range(3):
                part = jnp.dot(w_ref[a], s_ref[k, z + a], preferred_element_type=F32)
                total = part if total is None else total + part
            for d in range(n):
                for h in range(nh):
                    o_ref[d, k, z, h] = total[d * cg : (d + 1) * cg, h * w : (h + 1) * w]


def swap_all(array, axes):
    return lax.all_to_all(array, axes, 0, 0, tiled=True)


def step(activations, weight, grad_out):
    nz, rows, cg, w = activations.shape
    n = lax.axis_size(FILT)
    chips = lax.axis_size(CHIPS)
    ns = lax.axis_size(SPACE)
    ch = n * cg
    nr = rows // n + 2
    nh = nr - 2
    norm = float(nz * ns * rows * w) ** (-0.5)
    core = lax.axis_index("core").astype(jnp.int32).reshape(1)
    up = [(i, i + 1) for i in range(ns - 1)]
    down = [(j, i) for i, j in up]
    swap = [(0, 1), (1, 0)]
    sds = jax.ShapeDtypeStruct
    packed = [sds((n, nz, nr, cg, w), BF)]

    (px,) = call(pack_kernel, packed, [activations])
    x = swap_all(px, FILT)
    grad_out, px = lax.optimization_barrier((grad_out, px))
    (pg,) = call(pack_kernel, packed, [grad_out])
    g = swap_all(pg, FILT)

    flat_w = weight.transpose(0, 1, 2, 4, 3).reshape(27, cg, ch)
    flat_w, pg = lax.optimization_barrier((flat_w, pg))
    mine = swap_all(jnp.broadcast_to(flat_w[None], (chips, 27, cg, ch)), CHIPS)
    other = lax.ppermute(mine, "core", swap)
    wt, wf = call(weights_kernel, [sds((3, ch, 9 * ch), BF)] * 2, [core, mine, other], smem=1)

    xb = lax.ppermute(x[:, nz - 1], SPACE, up)
    xa = lax.ppermute(x[:, 0], SPACE, down)
    gb = lax.ppermute(g[:, nz - 1], SPACE, up)
    ga = lax.ppermute(g[:, 0], SPACE, down)

    any_spec = pl.BlockSpec(memory_space=pl.ANY)
    keep, send = pl.pallas_call(
        wgrad_kernel,
        out_shape=(sds((chips, 27, cg, ch), F32),) * 2,
        in_specs=[pl.BlockSpec(memory_space=pltpu.SMEM)] + vmem_specs(4),
        out_specs=(any_spec, any_spec),
        scratch_shapes=[
            pltpu.VMEM((nz + 2, 9 * ch, nh * w), BF),
            pltpu.VMEM((nz, ch, nh * w), BF),
            pltpu.VMEM((2, chips, 27, cg, ch), F32),
            pltpu.SemaphoreType.DMA((2,)),
        ],
        cost_estimate=pl.CostEstimate(
            flops=2 * 27 * ch * ch * nz * nh * w, transcendentals=0, bytes_accessed=4 * 27 * ch * ch
        ),
        name="wgrad",
    )(core, x, xb, xa, g)
    pair = keep + lax.ppermute(send, "core", swap)
    group = swap_all(pair, CHIPS).reshape(chips, 27, cg, ch).sum(0)

    (blocks,) = call(
        conv_kernel,
        [sds((n, 2, nz, nh, cg, w), F32)],
        [x, xb, xa, g, gb, ga, wt, wf],
        scratch=[pltpu.VMEM((2, nz + 2, 9 * ch, nh * w), BF)],
        flops=2 * 2 * 27 * ch * ch * nz * nh * w,
    )
    group, blocks = lax.optimization_barrier((group, blocks))
    back = swap_all(blocks, FILT)
    back = back.transpose(1, 2, 0, 3, 4, 5).reshape(2, nz, rows, cg, w)

    padded = jnp.pad(group, ((0, ns - 27), (0, 0), (0, 0)))
    shares = swap_all(padded, SPACE)
    tap = shares.sum(0) * norm
    taps = swap_all(jnp.broadcast_to(tap[None], (ns, cg, ch)), SPACE)
    weight_grad = taps[:27].reshape(3, 3, 3, cg, ch).transpose(0, 1, 2, 4, 3)
    return back[0], back[1], weight_grad


def solution(mesh):
    fine = Mesh(mesh.devices.reshape(8, 4, 2, 4, 2), SPACE + FILT)
    return jax.shard_map(
        step,
        mesh=fine,
        in_specs=(
            P(SPACE, None, FILT, None),
            P(None, None, None, None, FILT),
            P(SPACE, None, FILT, None),
        ),
        out_specs=(
            P(SPACE, None, FILT, None),
            P(SPACE, None, FILT, None),
            P(None, None, None, None, FILT),
        ),
        check_vma=False,
    )
```

```python
import jax
import jax.numpy as jnp
from jax import lax
from jax.experimental import pallas as pl
from jax.experimental.pallas import tpu as pltpu
from jax.sharding import Mesh
from jax.sharding import PartitionSpec as P


SPACE = ("y", "zh")
FILT = ("zl", "x", "core")
CHIPS = ("zl", "x")
BF, F32 = jnp.bfloat16, jnp.float32


def vmem_specs(n):
    return [pl.BlockSpec(memory_space=pltpu.VMEM)] * n


def call(kernel, outs, ins, scratch=(), smem=0, flops=0):
    specs = [pl.BlockSpec(memory_space=pltpu.SMEM)] * smem + vmem_specs(len(ins) - smem)
    moved = sum(a.size * a.dtype.itemsize for a in ins) + sum(o.size * o.dtype.itemsize for o in outs)
    return pl.pallas_call(
        kernel,
        out_shape=tuple(outs),
        in_specs=specs,
        out_specs=tuple(vmem_specs(len(outs))),
        scratch_shapes=list(scratch),
        cost_estimate=pl.CostEstimate(flops=flops, transcendentals=0, bytes_accessed=moved),
    )(*ins)


def pack_kernel(x_ref, g_ref, o_ref):
    n, _, nz, nr = o_ref.shape[:4]
    rows = x_ref.shape[1]
    zero = jnp.zeros(x_ref.shape[2:], x_ref.dtype)
    for k, ref in enumerate((x_ref, g_ref)):
        for z in range(nz):
            for d in range(n):
                for r in range(nr):
                    h = d * (nr - 2) + r - 1
                    o_ref[d, k, z, r] = ref[z, h] if 0 <= h < rows else zero


def pack_more_kernel(w_ref, before_ref, after_ref, o_ref):
    chips, total = o_ref.shape[:2]
    taps = w_ref.shape[0]
    rows = before_ref.shape[0]
    nr = (total - taps) // 2
    zero = jnp.zeros(w_ref.shape[1:], w_ref.dtype)
    for q in range(chips):
        for t in range(taps):
            o_ref[q, t] = w_ref[t]
        for p, ref in enumerate((before_ref, after_ref)):
            for r in range(nr):
                h = q * (nr - 2) + r - 1
                o_ref[q, taps + p * nr + r] = ref[h] if 0 <= h < rows else zero


def shifted(value):
    lane = lax.broadcasted_iota(jnp.int32, value.shape, 1)
    w = value.shape[1]
    left = jnp.where(lane == 0, 0.0, pltpu.roll(value, 1, 1))
    right = jnp.where(lane == w - 1, 0.0, pltpu.roll(value, w - 1, 1))
    return left.astype(BF), value.astype(BF), right.astype(BF)


def stack(parts):
    return jnp.concatenate([p.astype(F32) for p in parts], 0)


def by_core(first, mine, other):
    parts = []
    for m, o in zip(mine, other):
        m, o = m.astype(F32), o.astype(F32)
        parts += [jnp.where(first, m, o), jnp.where(first, o, m)]
    return jnp.concatenate(parts, 0)


def build(planes, sizes, s_ref):
    nr, ch, w = sizes
    for p, plane in enumerate(planes):
        for r in range(nr):
            for c, v in enumerate(shifted(plane(r))):
                for h in range(nr - 2):
                    b = r - h
                    if 0 <= b < 3:
                        s_ref[p, pl.ds((3 * b + c) * ch, ch), pl.ds(h * w, w)] = v


def own_plane(own_ref, k, z):
    return lambda r: stack([own_ref[d, k, z, r] for d in range(own_ref.shape[0])])


def halo_plane(ref):
    return lambda r: stack([ref[d, r] for d in range(ref.shape[0])])


def x_planes(own_ref, before_ref, after_ref):
    inner = [own_plane(own_ref, 0, z) for z in range(own_ref.shape[2])]
    return [halo_plane(before_ref)] + inner + [halo_plane(after_ref)]


def wgrad_kernel(core_ref, own_ref, before_ref, after_ref, keep_ref, send_ref, s_ref, t_ref, o_ref, sems):
    n, _, nz, nr, cg, w = own_ref.shape
    nh, ch = nr - 2, n * cg
    build(x_planes(own_ref, before_ref, after_ref), (nr, ch, w), s_ref)
    for z in range(nz):
        for h in range(nh):
            t_ref[z, :, pl.ds(h * w, w)] = own_plane(own_ref, 1, z)(h + 1).astype(BF)
    core = core_ref[0]
    for a in range(3):
        for b in range(3):
            total = None
            for z in range(nz):
                part = lax.dot_general(
                    t_ref[z],
                    s_ref[z + a, pl.ds(3 * b * ch, 3 * ch), :],
                    (((1,), (1,)), ((), ())),
                    preferred_element_type=F32,
                )
                total = part if total is None else total + part
            for c in range(3):
                for d in range(n):
                    slot = (d % 2) ^ core
                    o_ref[slot, d // 2, 9 * a + 3 * b + c] = total[d * cg : (d + 1) * cg, c * ch : (c + 1) * ch]
    copies = [
        pltpu.make_async_copy(o_ref.at[1], send_ref, sems.at[1]),
        pltpu.make_async_copy(o_ref.at[0], keep_ref, sems.at[0]),
    ]
    for copy in copies:
        copy.start()
    for copy in copies:
        copy.wait()


def conv_kernel(core_ref, own_ref, before_ref, after_ref, mine_ref, other_ref, o_ref, s_ref, wt_ref, wf_ref):
    n, _, nz, nr, cg, w = own_ref.shape
    nh, ch = nr - 2, n * cg
    chips, total = mine_ref.shape[:2]
    taps = 27
    span = (total - taps) // 2
    core = core_ref[0]
    first = core == 0
    for t in range(taps):
        a, bc = t // 9, t % 9
        block = by_core(first, [mine_ref[q, t] for q in range(chips)], [other_ref[q, t] for q in range(chips)])
        wt_ref[a, :, pl.ds(bc * ch, ch)] = block.astype(BF)
        wf_ref[2 - a, :, pl.ds((8 - bc) * ch, ch)] = block.T.astype(BF)

    def g_halo(p):
        def rows(r):
            i = taps + p * span + r + core * nh
            return by_core(first, [mine_ref[q, i] for q in range(chips)], [other_ref[q, i] for q in range(chips)])

        return rows

    g_planes = [g_halo(0)] + [own_plane(own_ref, 1, z) for z in range(nz)] + [g_halo(1)]
    build(x_planes(own_ref, before_ref, after_ref), (nr, ch, w), s_ref.at[0])
    build(g_planes, (nr, ch, w), s_ref.at[1])
    for k, w_ref in enumerate((wt_ref, wf_ref)):
        for z in range(nz):
            total = None
            for a in range(3):
                part = jnp.dot(w_ref[a], s_ref[k, z + a], preferred_element_type=F32)
                total = part if total is None else total + part
            for d in range(n):
                for h in range(nh):
                    o_ref[d, k, z, h] = total[d * cg : (d + 1) * cg, h * w : (h + 1) * w]


def swap_all(array, axes):
    return lax.all_to_all(array, axes, 0, 0, tiled=True)


def step(activations, weight, grad_out):
    nz, rows, cg, w = activations.shape
    n = lax.axis_size(FILT)
    chips = lax.axis_size(CHIPS)
    ns = lax.axis_size(SPACE)
    ch = n * cg
    nr = rows // n + 2
    nh = nr - 2
    norm = float(nz * ns * rows * w) ** (-0.5)
    core = lax.axis_index("core").astype(jnp.int32).reshape(1)
    up = [(i, i + 1) for i in range(ns - 1)]
    down = [(j, i) for i, j in up]
    swap = [(0, 1), (1, 0)]
    sds = jax.ShapeDtypeStruct
    gb = lax.ppermute(grad_out[nz - 1], SPACE, up)
    ga = lax.ppermute(grad_out[0], SPACE, down)
    (packed,) = call(pack_kernel, [sds((n, 2, nz, nr, cg, w), BF)], [activations, grad_out])
    own = swap_all(packed, FILT)
    xb = lax.ppermute(own[:, 0, nz - 1], SPACE, up)
    xa = lax.ppermute(own[:, 0, 0], SPACE, down)

    flat_w = weight.transpose(0, 1, 2, 4, 3).reshape(27, cg, ch)
    span = rows // chips + 2
    (more,) = call(pack_more_kernel, [sds((chips, 27 + 2 * span, cg, ch), BF)], [flat_w, gb, ga])
    mine = swap_all(more, CHIPS)
    other = lax.ppermute(mine, "core", swap)

    any_spec = pl.BlockSpec(memory_space=pl.ANY)
    keep, send = pl.pallas_call(
        wgrad_kernel,
        out_shape=(sds((chips, 27, cg, ch), F32),) * 2,
        in_specs=[pl.BlockSpec(memory_space=pltpu.SMEM)] + vmem_specs(3),
        out_specs=(any_spec, any_spec),
        scratch_shapes=[
            pltpu.VMEM((nz + 2, 9 * ch, nh * w), BF),
            pltpu.VMEM((nz, ch, nh * w), BF),
            pltpu.VMEM((2, chips, 27, cg, ch), F32),
            pltpu.SemaphoreType.DMA((2,)),
        ],
        cost_estimate=pl.CostEstimate(
            flops=2 * 27 * ch * ch * nz * nh * w, transcendentals=0, bytes_accessed=4 * 27 * ch * ch
        ),
        name="wgrad",
    )(core, own, xb, xa)
    pair = keep + lax.ppermute(send, "core", swap)
    group = swap_all(pair, CHIPS).reshape(chips, 27, cg, ch).sum(0)

    (blocks,) = call(
        conv_kernel,
        [sds((n, 2, nz, nh, cg, w), F32)],
        [core, own, xb, xa, mine, other],
        scratch=[pltpu.VMEM((2, nz + 2, 9 * ch, nh * w), BF)] + [pltpu.VMEM((3, ch, 9 * ch), BF)] * 2,
        smem=1,
        flops=2 * 2 * 27 * ch * ch * nz * nh * w,
    )
    group, blocks = lax.optimization_barrier((group, blocks))
    back = swap_all(blocks, FILT)
    back = back.transpose(1, 2, 0, 3, 4, 5).reshape(2, nz, rows, cg, w)

    padded = jnp.pad(group, ((0, ns - 27), (0, 0), (0, 0)))
    shares = swap_all(padded, SPACE)
    tap = shares.sum(0) * norm
    taps = swap_all(jnp.broadcast_to(tap[None], (ns, cg, ch)), SPACE)
    weight_grad = taps[:27].reshape(3, 3, 3, cg, ch).transpose(0, 1, 2, 4, 3)
    return back[0], back[1], weight_grad


def solution(mesh):
    fine = Mesh(mesh.devices.reshape(8, 4, 2, 4, 2), SPACE + FILT)
    return jax.shard_map(
        step,
        mesh=fine,
        in_specs=(
            P(SPACE, None, FILT, None),
            P(None, None, None, None, FILT),
            P(SPACE, None, FILT, None),
        ),
        out_specs=(
            P(SPACE, None, FILT, None),
            P(SPACE, None, FILT, None),
            P(None, None, None, None, FILT),
        ),
        check_vma=False,
    )
```

```python
import jax
import jax.numpy as jnp
from jax import lax
from jax.experimental import pallas as pl
from jax.experimental.pallas import tpu as pltpu
from jax.sharding import Mesh
from jax.sharding import PartitionSpec as P


SPACE = ("y", "zh")
FILT = ("zl", "x", "core")
CHIPS = ("zl", "x")
BF, F32 = jnp.bfloat16, jnp.float32


def vmem_specs(n):
    return [pl.BlockSpec(memory_space=pltpu.VMEM)] * n


def call(kernel, outs, ins, scratch=(), smem=0, flops=0):
    specs = [pl.BlockSpec(memory_space=pltpu.SMEM)] * smem + vmem_specs(len(ins) - smem)
    moved = sum(a.size * a.dtype.itemsize for a in ins) + sum(o.size * o.dtype.itemsize for o in outs)
    return pl.pallas_call(
        kernel,
        out_shape=tuple(outs),
        in_specs=specs,
        out_specs=tuple(vmem_specs(len(outs))),
        scratch_shapes=list(scratch),
        cost_estimate=pl.CostEstimate(flops=flops, transcendentals=0, bytes_accessed=moved),
    )(*ins)


def pack_kernel(x_ref, g_ref, o_ref):
    n, _, nz, nr = o_ref.shape[:4]
    rows = x_ref.shape[1]
    zero = jnp.zeros(x_ref.shape[2:], x_ref.dtype)
    for k, ref in enumerate((x_ref, g_ref)):
        for z in range(nz):
            for d in range(n):
                for r in range(nr):
                    h = d * (nr - 2) + r - 1
                    o_ref[d, k, z, r] = ref[z, h] if 0 <= h < rows else zero


def pack_more_kernel(w_ref, before_ref, after_ref, o_ref):
    chips, total = o_ref.shape[:2]
    taps = w_ref.shape[0]
    rows = before_ref.shape[0]
    nr = (total - taps) // 2
    zero = jnp.zeros(w_ref.shape[1:], w_ref.dtype)
    for q in range(chips):
        for t in range(taps):
            o_ref[q, t] = w_ref[t]
        for p, ref in enumerate((before_ref, after_ref)):
            for r in range(nr):
                h = q * (nr - 2) + r - 1
                o_ref[q, taps + p * nr + r] = ref[h] if 0 <= h < rows else zero


def shifted(value):
    lane = lax.broadcasted_iota(jnp.int32, value.shape, 1)
    w = value.shape[1]
    left = jnp.where(lane == 0, 0.0, pltpu.roll(value, 1, 1))
    right = jnp.where(lane == w - 1, 0.0, pltpu.roll(value, w - 1, 1))
    return left.astype(BF), value.astype(BF), right.astype(BF)


def stack(parts):
    return jnp.concatenate([p.astype(F32) for p in parts], 0)


def by_core(first, mine, other):
    parts = []
    for m, o in zip(mine, other):
        m, o = m.astype(F32), o.astype(F32)
        parts += [jnp.where(first, m, o), jnp.where(first, o, m)]
    return jnp.concatenate(parts, 0)


def build(planes, sizes, s_ref):
    nr, ch, w = sizes
    for p, plane in enumerate(planes):
        for r in range(nr):
            for c, v in enumerate(shifted(plane(r))):
                for h in range(nr - 2):
                    b = r - h
                    if 0 <= b < 3:
                        s_ref[p, pl.ds((3 * b + c) * ch, ch), pl.ds(h * w, w)] = v


def own_plane(own_ref, k, z):
    return lambda r: stack([own_ref[d, k, z, r] for d in range(own_ref.shape[0])])


def halo_plane(ref):
    return lambda r: stack([ref[d, r] for d in range(ref.shape[0])])


def x_planes(own_ref, before_ref, after_ref):
    inner = [own_plane(own_ref, 0, z) for z in range(own_ref.shape[2])]
    return [halo_plane(before_ref)] + inner + [halo_plane(after_ref)]


def wgrad_kernel(core_ref, own_ref, before_ref, after_ref, keep_ref, send_ref, s_ref, t_ref, o_ref, sems):
    n, _, nz, nr, cg, w = own_ref.shape
    nh, ch = nr - 2, n * cg
    build(x_planes(own_ref, before_ref, after_ref), (nr, ch, w), s_ref)
    for z in range(nz):
        for h in range(nh):
            t_ref[z, :, pl.ds(h * w, w)] = own_plane(own_ref, 1, z)(h + 1).astype(BF)
    core = core_ref[0]
    for a in range(3):
        for b in range(3):
            total = None
            for z in range(nz):
                part = lax.dot_general(
                    t_ref[z],
                    s_ref[z + a, pl.ds(3 * b * ch, 3 * ch), :],
                    (((1,), (1,)), ((), ())),
                    preferred_element_type=F32,
                )
                total = part if total is None else total + part
            for c in range(3):
                for d in range(n):
                    slot = (d % 2) ^ core
                    o_ref[slot, d // 2, 9 * a + 3 * b + c] = total[d * cg : (d + 1) * cg, c * ch : (c + 1) * ch]
    copies = [
        pltpu.make_async_copy(o_ref.at[1], send_ref, sems.at[1]),
        pltpu.make_async_copy(o_ref.at[0], keep_ref, sems.at[0]),
    ]
    for copy in copies:
        copy.start()
    for copy in copies:
        copy.wait()


def place_of(index):
    return index >> 3, (index >> 1) & 3, index & 1


def conv_kernel(
    f_ref, own_ref, before_ref, after_ref, mine_ref, other_ref, keep_ref, send_ref, s_ref, wt_ref, wf_ref, o_ref, sems
):
    n, _, nz, nr, cg, w = own_ref.shape
    nh, ch = nr - 2, n * cg
    chips, total = mine_ref.shape[:2]
    taps = 27
    span = (total - taps) // 2
    zl, x, core = place_of(f_ref[0])
    first = core == 0
    for t in range(taps):
        a, bc = t // 9, t % 9
        block = by_core(first, [mine_ref[q, t] for q in range(chips)], [other_ref[q, t] for q in range(chips)])
        wt_ref[a, :, pl.ds(bc * ch, ch)] = block.astype(BF)
        wf_ref[2 - a, :, pl.ds((8 - bc) * ch, ch)] = block.T.astype(BF)

    def g_halo(p):
        def rows(r):
            i = taps + p * span + r + core * nh
            return by_core(first, [mine_ref[q, i] for q in range(chips)], [other_ref[q, i] for q in range(chips)])

        return rows

    g_planes = [g_halo(0)] + [own_plane(own_ref, 1, z) for z in range(nz)] + [g_halo(1)]
    build(x_planes(own_ref, before_ref, after_ref), (nr, ch, w), s_ref.at[0])
    build(g_planes, (nr, ch, w), s_ref.at[1])
    for k, w_ref in enumerate((wt_ref, wf_ref)):
        for z in range(nz):
            total = None
            for a in range(3):
                part = jnp.dot(w_ref[a], s_ref[k, z + a], preferred_element_type=F32)
                total = part if total is None else total + part
            for d in range(n):
                dzl, dx, dcore = place_of(d)
                slot = (dcore ^ core, dzl ^ zl, (dx - x) & 3)
                for h in range(nh):
                    o_ref[(*slot, k, z, h)] = total[d * cg : (d + 1) * cg, h * w : (h + 1) * w]
    copies = [
        pltpu.make_async_copy(o_ref.at[1], send_ref, sems.at[1]),
        pltpu.make_async_copy(o_ref.at[0], keep_ref, sems.at[0]),
    ]
    for copy in copies:
        copy.start()
    for copy in copies:
        copy.wait()


def place_kernel(f_ref, *refs):
    parts, outs = refs[:-2], refs[-2:]
    zl, x, core = place_of(f_ref[0])
    for dx, ref in enumerate(parts):
        for j in range(ref.shape[0]):
            source = ((zl ^ (j >> 1)) * 4 + ((x - dx) & 3)) * 2 + (core ^ (j & 1))
            for k, o_ref in enumerate(outs):
                for z in range(ref.shape[2]):
                    for h in range(ref.shape[3]):
                        o_ref[z, source * ref.shape[3] + h] = ref[j, k, z, h]


def swap_all(array, axes):
    return lax.all_to_all(array, axes, 0, 0, tiled=True)


def step(activations, weight, grad_out):
    nz, rows, cg, w = activations.shape
    n = lax.axis_size(FILT)
    chips = lax.axis_size(CHIPS)
    ns = lax.axis_size(SPACE)
    ch = n * cg
    nr = rows // n + 2
    nh = nr - 2
    norm = float(nz * ns * rows * w) ** (-0.5)
    core = lax.axis_index("core").astype(jnp.int32).reshape(1)
    up = [(i, i + 1) for i in range(ns - 1)]
    down = [(j, i) for i, j in up]
    swap = [(0, 1), (1, 0)]
    sds = jax.ShapeDtypeStruct
    gb = lax.ppermute(grad_out[nz - 1], SPACE, up)
    ga = lax.ppermute(grad_out[0], SPACE, down)
    (packed,) = call(pack_kernel, [sds((n, 2, nz, nr, cg, w), BF)], [activations, grad_out])
    own = swap_all(packed, FILT)
    xb = lax.ppermute(own[:, 0, nz - 1], SPACE, up)
    xa = lax.ppermute(own[:, 0, 0], SPACE, down)

    flat_w = weight.transpose(0, 1, 2, 4, 3).reshape(27, cg, ch)
    span = rows // chips + 2
    (more,) = call(pack_more_kernel, [sds((chips, 27 + 2 * span, cg, ch), BF)], [flat_w, gb, ga])
    mine = swap_all(more, CHIPS)
    other = lax.ppermute(mine, "core", swap)

    any_spec = pl.BlockSpec(memory_space=pl.ANY)
    keep, send = pl.pallas_call(
        wgrad_kernel,
        out_shape=(sds((chips, 27, cg, ch), F32),) * 2,
        in_specs=[pl.BlockSpec(memory_space=pltpu.SMEM)] + vmem_specs(3),
        out_specs=(any_spec, any_spec),
        scratch_shapes=[
            pltpu.VMEM((nz + 2, 9 * ch, nh * w), BF),
            pltpu.VMEM((nz, ch, nh * w), BF),
            pltpu.VMEM((2, chips, 27, cg, ch), F32),
            pltpu.SemaphoreType.DMA((2,)),
        ],
        cost_estimate=pl.CostEstimate(
            flops=2 * 27 * ch * ch * nz * nh * w, transcendentals=0, bytes_accessed=4 * 27 * ch * ch
        ),
        name="wgrad",
    )(core, own, xb, xa)
    pair = keep + lax.ppermute(send, "core", swap)
    pieces = swap_all(pair, CHIPS).reshape(chips, 27, cg, ch)
    group = pieces.sum(0)

    index = lax.axis_index(FILT).astype(jnp.int32).reshape(1)
    keep, send = pl.pallas_call(
        conv_kernel,
        out_shape=(sds((2, 4, 2, nz, nh, cg, w), F32),) * 2,
        in_specs=[pl.BlockSpec(memory_space=pltpu.SMEM)] + vmem_specs(5),
        out_specs=(any_spec, any_spec),
        scratch_shapes=[
            pltpu.VMEM((2, nz + 2, 9 * ch, nh * w), BF),
            pltpu.VMEM((3, ch, 9 * ch), BF),
            pltpu.VMEM((3, ch, 9 * ch), BF),
            pltpu.VMEM((2, 2, 4, 2, nz, nh, cg, w), F32),
            pltpu.SemaphoreType.DMA((2,)),
        ],
        cost_estimate=pl.CostEstimate(
            flops=4 * 27 * ch * ch * nz * nh * w, transcendentals=0, bytes_accessed=4 * 27 * ch * ch
        ),
        name="conv",
    )(index, own, xb, xa, mine, other)
    got = lax.ppermute(send, "core", swap)
    far = lax.ppermute(jnp.stack([keep[1], got[1]]), "zl", swap)
    blocks = [jnp.stack([keep[0, j], got[0, j], far[0, j], far[1, j]]) for j in range(4)]
    blocks = blocks[:1] + [
        lax.ppermute(blocks[j], "x", [(i, (i + j) % 4) for i in range(4)]) for j in range(1, 4)
    ]
    output, grad_in = call(place_kernel, [sds((nz, rows, cg, w), F32)] * 2, [index, *blocks], smem=1)

    padded = jnp.pad(group, ((0, ns - 27), (0, 0), (0, 0)))
    shares = swap_all(padded, SPACE)
    tap = shares.sum(0) * norm
    taps = swap_all(jnp.broadcast_to(tap[None], (ns, cg, ch)), SPACE)
    weight_grad = taps[:27].reshape(3, 3, 3, cg, ch).transpose(0, 1, 2, 4, 3)
    return output, grad_in, weight_grad


def solution(mesh):
    fine = Mesh(mesh.devices.reshape(8, 4, 2, 4, 2), SPACE + FILT)
    return jax.shard_map(
        step,
        mesh=fine,
        in_specs=(
            P(SPACE, None, FILT, None),
            P(None, None, None, None, FILT),
            P(SPACE, None, FILT, None),
        ),
        out_specs=(
            P(SPACE, None, FILT, None),
            P(SPACE, None, FILT, None),
            P(None, None, None, None, FILT),
        ),
        check_vma=False,
    )
```

```python
import jax
import jax.numpy as jnp
from jax import lax
from jax.experimental import pallas as pl
from jax.experimental.pallas import tpu as pltpu
from jax.sharding import Mesh
from jax.sharding import PartitionSpec as P


SPACE = ("y", "zh")
FILT = ("zl", "x", "core")
CHIPS = ("zl", "x")
BF, F32 = jnp.bfloat16, jnp.float32


def vmem_specs(n):
    return [pl.BlockSpec(memory_space=pltpu.VMEM)] * n


def call(kernel, outs, ins, scratch=(), smem=0, flops=0):
    specs = [pl.BlockSpec(memory_space=pltpu.SMEM)] * smem + vmem_specs(len(ins) - smem)
    moved = sum(a.size * a.dtype.itemsize for a in ins) + sum(o.size * o.dtype.itemsize for o in outs)
    return pl.pallas_call(
        kernel,
        out_shape=tuple(outs),
        in_specs=specs,
        out_specs=tuple(vmem_specs(len(outs))),
        scratch_shapes=list(scratch),
        cost_estimate=pl.CostEstimate(flops=flops, transcendentals=0, bytes_accessed=moved),
    )(*ins)


def place_of(index):
    return (index >> 3) & 1, (index >> 1) & 3, index & 1


def odd_slab(index):
    return (index >> 4) & 1 == 1


def pack_kernel(x_ref, g_ref, o_ref):
    n, _, nz, nr = o_ref.shape[:4]
    rows = x_ref.shape[1]
    zero = jnp.zeros(x_ref.shape[2:], x_ref.dtype)
    for k, ref in enumerate((x_ref, g_ref)):
        for z in range(nz):
            for d in range(n):
                for r in range(nr):
                    h = d * (nr - 2) + r - 1
                    o_ref[d, k, z, r] = ref[z, h] if 0 <= h < rows else zero


def halo_pick(index):
    odd = odd_slab(index)

    def pick(side, even, odd_side):
        even, odd_side = even.astype(F32), odd_side.astype(F32)
        return jnp.where(odd == (side == 0), even, odd_side).astype(BF)

    return pick


def pack_more_kernel(p_ref, w_ref, even_ref, odd_ref, o_ref):
    chips, total = o_ref.shape[:2]
    taps = w_ref.shape[0]
    rows = even_ref.shape[0]
    nr = (total - taps) // 2
    pick = halo_pick(p_ref[0])
    zero = jnp.zeros(w_ref.shape[1:], w_ref.dtype)
    for q in range(chips):
        for t in range(taps):
            o_ref[q, t] = w_ref[t]
        for p in range(2):
            for r in range(nr):
                h = q * (nr - 2) + r - 1
                o_ref[q, taps + p * nr + r] = pick(p, even_ref[h], odd_ref[h]) if 0 <= h < rows else zero


def shifted(value):
    lane = lax.broadcasted_iota(jnp.int32, value.shape, 1)
    w = value.shape[1]
    left = jnp.where(lane == 0, 0.0, pltpu.roll(value, 1, 1))
    right = jnp.where(lane == w - 1, 0.0, pltpu.roll(value, w - 1, 1))
    return left.astype(BF), value.astype(BF), right.astype(BF)


def stack(parts):
    return jnp.concatenate([p.astype(F32) for p in parts], 0)


def by_core(first, mine, other):
    parts = []
    for m, o in zip(mine, other):
        m, o = m.astype(F32), o.astype(F32)
        parts += [jnp.where(first, m, o), jnp.where(first, o, m)]
    return jnp.concatenate(parts, 0)


def build(planes, sizes, s_ref):
    nr, ch, w = sizes
    for p, plane in enumerate(planes):
        for r in range(nr):
            for c, v in enumerate(shifted(plane(r))):
                for h in range(nr - 2):
                    b = r - h
                    if 0 <= b < 3:
                        s_ref[p, pl.ds((3 * b + c) * ch, ch), pl.ds(h * w, w)] = v


def own_plane(own_ref, k, z):
    return lambda r: stack([own_ref[d, k, z, r] for d in range(own_ref.shape[0])])


def halo_plane(index, side, even_ref, odd_ref):
    take_even = odd_slab(index) == (side == 0)

    def rows(r):
        n = even_ref.shape[0]
        return jnp.where(take_even, stack([even_ref[d, r] for d in range(n)]), stack([odd_ref[d, r] for d in range(n)]))

    return rows


def x_planes(index, own_ref, even_ref, odd_ref):
    inner = [own_plane(own_ref, 0, z) for z in range(own_ref.shape[2])]
    return [halo_plane(index, 0, even_ref, odd_ref)] + inner + [halo_plane(index, 1, even_ref, odd_ref)]


def wgrad_kernel(p_ref, own_ref, even_ref, odd_ref, keep_ref, send_ref, s_ref, t_ref, o_ref, sems):
    n, _, nz, nr, cg, w = own_ref.shape
    nh, ch = nr - 2, n * cg
    build(x_planes(p_ref[0], own_ref, even_ref, odd_ref), (nr, ch, w), s_ref)
    for z in range(nz):
        for h in range(nh):
            t_ref[z, :, pl.ds(h * w, w)] = own_plane(own_ref, 1, z)(h + 1).astype(BF)
    core = place_of(p_ref[0])[2]
    for a in range(3):
        for b in range(3):
            total = None
            for z in range(nz):
                part = lax.dot_general(
                    t_ref[z],
                    s_ref[z + a, pl.ds(3 * b * ch, 3 * ch), :],
                    (((1,), (1,)), ((), ())),
                    preferred_element_type=F32,
                )
                total = part if total is None else total + part
            for c in range(3):
                for d in range(n):
                    slot = (d % 2) ^ core
                    o_ref[slot, d // 2, 9 * a + 3 * b + c] = total[d * cg : (d + 1) * cg, c * ch : (c + 1) * ch]
    copies = [
        pltpu.make_async_copy(o_ref.at[1], send_ref, sems.at[1]),
        pltpu.make_async_copy(o_ref.at[0], keep_ref, sems.at[0]),
    ]
    for copy in copies:
        copy.start()
    for copy in copies:
        copy.wait()


def conv_kernel(
    p_ref, own_ref, even_ref, odd_ref, mine_ref, other_ref, keep_ref, send_ref, s_ref, wt_ref, wf_ref, o_ref, sems
):
    n, _, nz, nr, cg, w = own_ref.shape
    nh, ch = nr - 2, n * cg
    chips, total = mine_ref.shape[:2]
    taps = 27
    span = (total - taps) // 2
    zl, x, core = place_of(p_ref[0])
    first = core == 0
    for t in range(taps):
        a, bc = t // 9, t % 9
        block = by_core(first, [mine_ref[q, t] for q in range(chips)], [other_ref[q, t] for q in range(chips)])
        wt_ref[a, :, pl.ds(bc * ch, ch)] = block.astype(BF)
        wf_ref[2 - a, :, pl.ds((8 - bc) * ch, ch)] = block.T.astype(BF)

    def g_halo(p):
        def rows(r):
            i = taps + p * span + r + core * nh
            return by_core(first, [mine_ref[q, i] for q in range(chips)], [other_ref[q, i] for q in range(chips)])

        return rows

    g_planes = [g_halo(0)] + [own_plane(own_ref, 1, z) for z in range(nz)] + [g_halo(1)]
    build(x_planes(p_ref[0], own_ref, even_ref, odd_ref), (nr, ch, w), s_ref.at[0])
    build(g_planes, (nr, ch, w), s_ref.at[1])
    for k, w_ref in enumerate((wt_ref, wf_ref)):
        for z in range(nz):
            total = None
            for a in range(3):
                part = jnp.dot(w_ref[a], s_ref[k, z + a], preferred_element_type=F32)
                total = part if total is None else total + part
            for d in range(n):
                dzl, dx, dcore = place_of(d)
                slot = (dcore ^ core, dzl ^ zl, dx ^ x)
                for h in range(nh):
                    o_ref[(*slot, k, z, h)] = total[d * cg : (d + 1) * cg, h * w : (h + 1) * w]
    copies = [
        pltpu.make_async_copy(o_ref.at[1], send_ref, sems.at[1]),
        pltpu.make_async_copy(o_ref.at[0], keep_ref, sems.at[0]),
    ]
    for copy in copies:
        copy.start()
    for copy in copies:
        copy.wait()


def place_kernel(p_ref, *refs):
    parts, outs = refs[:-2], refs[-2:]
    zl, x, core = place_of(p_ref[0])
    for dx, ref in enumerate(parts):
        for j in range(ref.shape[0]):
            source = ((zl ^ (j >> 1)) * 4 + (x ^ dx)) * 2 + (core ^ (j & 1))
            for k, o_ref in enumerate(outs):
                for z in range(ref.shape[2]):
                    for h in range(ref.shape[3]):
                        o_ref[z, source * ref.shape[3] + h] = ref[j, k, z, h]


def swap_all(array, axes):
    return lax.all_to_all(array, axes, 0, 0, tiled=True)


def step(activations, weight, grad_out):
    nz, rows, cg, w = activations.shape
    n = lax.axis_size(FILT)
    chips = lax.axis_size(CHIPS)
    ns = lax.axis_size(SPACE)
    ch = n * cg
    nr = rows // n + 2
    nh = nr - 2
    norm = float(nz * ns * rows * w) ** (-0.5)
    index = lax.axis_index(SPACE + FILT).astype(jnp.int32).reshape(1)
    parity = lax.axis_index(SPACE).astype(jnp.int32) & 1
    sides = [(nz - 1) * (1 - parity), (nz - 1) * parity]
    pairs = [[(i, i + 1) for i in range(first, ns - 1, 2)] for first in (0, 1)]
    pairs = [p + [(j, i) for i, j in p] for p in pairs]
    swap = [(0, 1), (1, 0)]
    sds = jax.ShapeDtypeStruct
    g_halos = [
        lax.ppermute(lax.dynamic_slice(grad_out, (side, 0, 0, 0), (1, rows, cg, w))[0], SPACE, pair)
        for side, pair in zip(sides, pairs)
    ]
    (packed,) = call(pack_kernel, [sds((n, 2, nz, nr, cg, w), BF)], [activations, grad_out])
    own = swap_all(packed, FILT)
    x_halos = [
        lax.ppermute(
            lax.dynamic_slice(own, (0, 0, side, 0, 0, 0), (n, 1, 1, nr, cg, w))[:, 0, 0], SPACE, pair
        )
        for side, pair in zip(sides, pairs)
    ]

    flat_w = weight.transpose(0, 1, 2, 4, 3).reshape(27, cg, ch)
    span = rows // chips + 2
    (more,) = call(pack_more_kernel, [sds((chips, 27 + 2 * span, cg, ch), BF)], [index, flat_w, *g_halos], smem=1)
    mine = swap_all(more, CHIPS)
    other = lax.ppermute(mine, "core", swap)

    any_spec = pl.BlockSpec(memory_space=pl.ANY)
    keep, send = pl.pallas_call(
        wgrad_kernel,
        out_shape=(sds((chips, 27, cg, ch), F32),) * 2,
        in_specs=[pl.BlockSpec(memory_space=pltpu.SMEM)] + vmem_specs(3),
        out_specs=(any_spec, any_spec),
        scratch_shapes=[
            pltpu.VMEM((nz + 2, 9 * ch, nh * w), BF),
            pltpu.VMEM((nz, ch, nh * w), BF),
            pltpu.VMEM((2, chips, 27, cg, ch), F32),
            pltpu.SemaphoreType.DMA((2,)),
        ],
        cost_estimate=pl.CostEstimate(
            flops=2 * 27 * ch * ch * nz * nh * w, transcendentals=0, bytes_accessed=4 * 27 * ch * ch
        ),
        name="wgrad",
    )(index, own, *x_halos)
    pair = keep + lax.ppermute(send, "core", swap)
    pieces = swap_all(pair, CHIPS).reshape(chips, 27, cg, ch)
    group = pieces.sum(0)

    keep, send = pl.pallas_call(
        conv_kernel,
        out_shape=(sds((2, 4, 2, nz, nh, cg, w), F32),) * 2,
        in_specs=[pl.BlockSpec(memory_space=pltpu.SMEM)] + vmem_specs(5),
        out_specs=(any_spec, any_spec),
        scratch_shapes=[
            pltpu.VMEM((2, nz + 2, 9 * ch, nh * w), BF),
            pltpu.VMEM((3, ch, 9 * ch), BF),
            pltpu.VMEM((3, ch, 9 * ch), BF),
            pltpu.VMEM((2, 2, 4, 2, nz, nh, cg, w), F32),
            pltpu.SemaphoreType.DMA((2,)),
        ],
        cost_estimate=pl.CostEstimate(
            flops=4 * 27 * ch * ch * nz * nh * w, transcendentals=0, bytes_accessed=4 * 27 * ch * ch
        ),
        name="conv",
    )(index, own, *x_halos, mine, other)
    got = lax.ppermute(send, "core", swap)
    group, got = lax.optimization_barrier((group, got))
    far = lax.ppermute(jnp.stack([keep[1], got[1]]), "zl", swap)
    blocks = [jnp.stack([keep[0, j], got[0, j], far[0, j], far[1, j]]) for j in range(4)]
    blocks = blocks[:1] + [
        lax.ppermute(blocks[j], "x", [(i, i ^ j) for i in range(4)]) for j in range(1, 4)
    ]
    output, grad_in = call(place_kernel, [sds((nz, rows, cg, w), F32)] * 2, [index, *blocks], smem=1)

    padded = jnp.pad(group, ((0, ns - 27), (0, 0), (0, 0)))
    shares = swap_all(padded, SPACE)
    tap = shares.sum(0) * norm
    taps = swap_all(jnp.broadcast_to(tap[None], (ns, cg, ch)), SPACE)
    weight_grad = taps[:27].reshape(3, 3, 3, cg, ch).transpose(0, 1, 2, 4, 3)
    return output, grad_in, weight_grad


def solution(mesh):
    fine = Mesh(mesh.devices.reshape(8, 4, 2, 4, 2), SPACE + FILT)
    return jax.shard_map(
        step,
        mesh=fine,
        in_specs=(
            P(SPACE, None, FILT, None),
            P(None, None, None, None, FILT),
            P(SPACE, None, FILT, None),
        ),
        out_specs=(
            P(SPACE, None, FILT, None),
            P(SPACE, None, FILT, None),
            P(None, None, None, None, FILT),
        ),
        check_vma=False,
    )
```

```python
import jax
import jax.numpy as jnp
from jax import lax
from jax.experimental import pallas as pl
from jax.experimental.pallas import tpu as pltpu
from jax.sharding import Mesh
from jax.sharding import PartitionSpec as P


SPACE = ("y", "zh")
FILT = ("zl", "x", "core")
CHIPS = ("zl", "x")
BF, F32 = jnp.bfloat16, jnp.float32


def vmem_specs(n):
    return [pl.BlockSpec(memory_space=pltpu.VMEM)] * n


def call(kernel, outs, ins, scratch=(), smem=0, flops=0):
    specs = [pl.BlockSpec(memory_space=pltpu.SMEM)] * smem + vmem_specs(len(ins) - smem)
    moved = sum(a.size * a.dtype.itemsize for a in ins) + sum(o.size * o.dtype.itemsize for o in outs)
    return pl.pallas_call(
        kernel,
        out_shape=tuple(outs),
        in_specs=specs,
        out_specs=tuple(vmem_specs(len(outs))),
        scratch_shapes=list(scratch),
        cost_estimate=pl.CostEstimate(flops=flops, transcendentals=0, bytes_accessed=moved),
    )(*ins)


def place_of(index):
    return (index >> 3) & 1, (index >> 1) & 3, index & 1


def odd_slab(index):
    return (index >> 4) & 1 == 1


def pack_kernel(x_ref, g_ref, o_ref):
    n, _, nz, nr = o_ref.shape[:4]
    rows = x_ref.shape[1]
    zero = jnp.zeros(x_ref.shape[2:], x_ref.dtype)
    for k, ref in enumerate((x_ref, g_ref)):
        for z in range(nz):
            for d in range(n):
                for r in range(nr):
                    h = d * (nr - 2) + r - 1
                    o_ref[d, k, z, r] = ref[z, h] if 0 <= h < rows else zero


def halo_pick(index):
    odd = odd_slab(index)

    def pick(side, even, odd_side):
        even, odd_side = even.astype(F32), odd_side.astype(F32)
        return jnp.where(odd == (side == 0), even, odd_side).astype(BF)

    return pick


def pack_more_kernel(p_ref, w_ref, even_ref, odd_ref, o_ref):
    chips, total = o_ref.shape[:2]
    taps = w_ref.shape[0]
    rows = even_ref.shape[0]
    nr = (total - taps) // 2
    pick = halo_pick(p_ref[0])
    zero = jnp.zeros(w_ref.shape[1:], w_ref.dtype)
    for q in range(chips):
        for t in range(taps):
            o_ref[q, t] = w_ref[t]
        for p in range(2):
            for r in range(nr):
                h = q * (nr - 2) + r - 1
                o_ref[q, taps + p * nr + r] = pick(p, even_ref[h], odd_ref[h]) if 0 <= h < rows else zero


def shifted(value):
    lane = lax.broadcasted_iota(jnp.int32, value.shape, 1)
    w = value.shape[1]
    left = jnp.where(lane == 0, 0.0, pltpu.roll(value, 1, 1))
    right = jnp.where(lane == w - 1, 0.0, pltpu.roll(value, w - 1, 1))
    return left.astype(BF), value.astype(BF), right.astype(BF)


def stack(parts):
    return jnp.concatenate([p.astype(F32) for p in parts], 0)


def by_core(first, mine, other):
    parts = []
    for m, o in zip(mine, other):
        m, o = m.astype(F32), o.astype(F32)
        parts += [jnp.where(first, m, o), jnp.where(first, o, m)]
    return jnp.concatenate(parts, 0)


def build(planes, sizes, s_ref):
    nr, ch, w = sizes
    for p, plane in enumerate(planes):
        for r in range(nr):
            for c, v in enumerate(shifted(plane(r))):
                for h in range(nr - 2):
                    b = r - h
                    if 0 <= b < 3:
                        s_ref[p, pl.ds((3 * b + c) * ch, ch), pl.ds(h * w, w)] = v


def own_plane(own_ref, k, z):
    return lambda r: stack([own_ref[d, k, z, r] for d in range(own_ref.shape[0])])


def halo_plane(index, side, even_ref, odd_ref):
    take_even = odd_slab(index) == (side == 0)

    def rows(r):
        n = even_ref.shape[0]
        return jnp.where(take_even, stack([even_ref[d, r] for d in range(n)]), stack([odd_ref[d, r] for d in range(n)]))

    return rows


def x_planes(index, own_ref, even_ref, odd_ref):
    inner = [own_plane(own_ref, 0, z) for z in range(own_ref.shape[2])]
    return [halo_plane(index, 0, even_ref, odd_ref)] + inner + [halo_plane(index, 1, even_ref, odd_ref)]


def wgrad_kernel(p_ref, own_ref, even_ref, odd_ref, keep_ref, send_ref, s_ref, t_ref, o_ref, sems):
    n, _, nz, nr, cg, w = own_ref.shape
    nh, ch = nr - 2, n * cg
    build(x_planes(p_ref[0], own_ref, even_ref, odd_ref), (nr, ch, w), s_ref)
    for z in range(nz):
        for h in range(nh):
            t_ref[z, :, pl.ds(h * w, w)] = own_plane(own_ref, 1, z)(h + 1).astype(BF)
    core = place_of(p_ref[0])[2]
    for a in range(3):
        for b in range(3):
            total = None
            for z in range(nz):
                part = lax.dot_general(
                    t_ref[z],
                    s_ref[z + a, pl.ds(3 * b * ch, 3 * ch), :],
                    (((1,), (1,)), ((), ())),
                    preferred_element_type=F32,
                )
                total = part if total is None else total + part
            for c in range(3):
                for d in range(n):
                    slot = (d % 2) ^ core
                    o_ref[slot, d // 2, 9 * a + 3 * b + c] = total[d * cg : (d + 1) * cg, c * ch : (c + 1) * ch]
    copies = [
        pltpu.make_async_copy(o_ref.at[1], send_ref, sems.at[1]),
        pltpu.make_async_copy(o_ref.at[0], keep_ref, sems.at[0]),
    ]
    for copy in copies:
        copy.start()
    for copy in copies:
        copy.wait()


def conv_kernel(
    p_ref, own_ref, even_ref, odd_ref, mine_ref, other_ref, out0, out1, out2, out3, s_ref, wt_ref, wf_ref, o_ref, sems
):
    n, _, nz, nr, cg, w = own_ref.shape
    nh, ch = nr - 2, n * cg
    chips, total = mine_ref.shape[:2]
    taps = 27
    span = (total - taps) // 2
    zl, x, core = place_of(p_ref[0])
    first = core == 0
    for t in range(taps):
        a, bc = t // 9, t % 9
        block = by_core(first, [mine_ref[q, t] for q in range(chips)], [other_ref[q, t] for q in range(chips)])
        wt_ref[a, :, pl.ds(bc * ch, ch)] = block.astype(BF)
        wf_ref[2 - a, :, pl.ds((8 - bc) * ch, ch)] = block.T.astype(BF)

    def g_halo(p):
        def rows(r):
            i = taps + p * span + r + core * nh
            return by_core(first, [mine_ref[q, i] for q in range(chips)], [other_ref[q, i] for q in range(chips)])

        return rows

    g_planes = [g_halo(0)] + [own_plane(own_ref, 1, z) for z in range(nz)] + [g_halo(1)]
    build(x_planes(p_ref[0], own_ref, even_ref, odd_ref), (nr, ch, w), s_ref.at[0])
    build(g_planes, (nr, ch, w), s_ref.at[1])
    for k, w_ref in enumerate((wt_ref, wf_ref)):
        for z in range(nz):
            total = None
            for a in range(3):
                part = jnp.dot(w_ref[a], s_ref[k, z + a], preferred_element_type=F32)
                total = part if total is None else total + part
            for d in range(n):
                dzl, dx, dcore = place_of(d)
                slot = (2 * (dzl ^ zl) + (dcore ^ core), dx ^ x)
                for h in range(nh):
                    o_ref[(*slot, k, z, h)] = total[d * cg : (d + 1) * cg, h * w : (h + 1) * w]
    copies = [pltpu.make_async_copy(o_ref.at[j], ref, sems.at[j]) for j, ref in enumerate((out0, out1, out2, out3))]
    for copy in copies:
        copy.start()
    for copy in copies:
        copy.wait()


def place_kernel(p_ref, *refs):
    parts, outs = refs[:-2], refs[-2:]
    zl, x, core = place_of(p_ref[0])
    for dx, ref in enumerate(parts):
        for j in range(ref.shape[0]):
            source = ((zl ^ (j >> 1)) * 4 + (x ^ dx)) * 2 + (core ^ (j & 1))
            for k, o_ref in enumerate(outs):
                for z in range(ref.shape[2]):
                    for h in range(ref.shape[3]):
                        o_ref[z, source * ref.shape[3] + h] = ref[j, k, z, h]


def swap_all(array, axes):
    return lax.all_to_all(array, axes, 0, 0, tiled=True)


def step(activations, weight, grad_out):
    nz, rows, cg, w = activations.shape
    n = lax.axis_size(FILT)
    chips = lax.axis_size(CHIPS)
    ns = lax.axis_size(SPACE)
    ch = n * cg
    nr = rows // n + 2
    nh = nr - 2
    norm = float(nz * ns * rows * w) ** (-0.5)
    index = lax.axis_index(SPACE + FILT).astype(jnp.int32).reshape(1)
    parity = lax.axis_index(SPACE).astype(jnp.int32) & 1
    sides = [(nz - 1) * (1 - parity), (nz - 1) * parity]
    pairs = [[(i, i + 1) for i in range(first, ns - 1, 2)] for first in (0, 1)]
    pairs = [p + [(j, i) for i, j in p] for p in pairs]
    swap = [(0, 1), (1, 0)]
    sds = jax.ShapeDtypeStruct
    g_halos = [
        lax.ppermute(lax.dynamic_slice(grad_out, (side, 0, 0, 0), (1, rows, cg, w))[0], SPACE, pair)
        for side, pair in zip(sides, pairs)
    ]
    (packed,) = call(pack_kernel, [sds((n, 2, nz, nr, cg, w), BF)], [activations, grad_out])
    own = swap_all(packed, FILT)
    x_halos = [
        lax.ppermute(
            lax.dynamic_slice(own, (0, 0, side, 0, 0, 0), (n, 1, 1, nr, cg, w))[:, 0, 0], SPACE, pair
        )
        for side, pair in zip(sides, pairs)
    ]

    flat_w = weight.transpose(0, 1, 2, 4, 3).reshape(27, cg, ch)
    span = rows // chips + 2
    (more,) = call(pack_more_kernel, [sds((chips, 27 + 2 * span, cg, ch), BF)], [index, flat_w, *g_halos], smem=1)
    mine = swap_all(more, CHIPS)
    other = lax.ppermute(mine, "core", swap)

    any_spec = pl.BlockSpec(memory_space=pl.ANY)
    keep, send = pl.pallas_call(
        wgrad_kernel,
        out_shape=(sds((chips, 27, cg, ch), F32),) * 2,
        in_specs=[pl.BlockSpec(memory_space=pltpu.SMEM)] + vmem_specs(3),
        out_specs=(any_spec, any_spec),
        scratch_shapes=[
            pltpu.VMEM((nz + 2, 9 * ch, nh * w), BF),
            pltpu.VMEM((nz, ch, nh * w), BF),
            pltpu.VMEM((2, chips, 27, cg, ch), F32),
            pltpu.SemaphoreType.DMA((2,)),
        ],
        cost_estimate=pl.CostEstimate(
            flops=2 * 27 * ch * ch * nz * nh * w, transcendentals=0, bytes_accessed=4 * 27 * ch * ch
        ),
        name="wgrad",
    )(index, own, *x_halos)
    got = lax.ppermute(send, "core", swap)
    pair = keep + got
    pieces = swap_all(pair, CHIPS).reshape(chips, 27, cg, ch)
    group = pieces.sum(0)

    near = pl.pallas_call(
        conv_kernel,
        out_shape=(sds((4, 2, nz, nh, cg, w), F32),) * 4,
        in_specs=[pl.BlockSpec(memory_space=pltpu.SMEM)] + vmem_specs(5),
        out_specs=(any_spec,) * 4,
        scratch_shapes=[
            pltpu.VMEM((2, nz + 2, 9 * ch, nh * w), BF),
            pltpu.VMEM((3, ch, 9 * ch), BF),
            pltpu.VMEM((3, ch, 9 * ch), BF),
            pltpu.VMEM((4, 4, 2, nz, nh, cg, w), F32),
            pltpu.SemaphoreType.DMA((4,)),
        ],
        cost_estimate=pl.CostEstimate(
            flops=4 * 27 * ch * ch * nz * nh * w, transcendentals=0, bytes_accessed=4 * 27 * ch * ch
        ),
        name="conv",
    )(index, own, *x_halos, mine, other)
    near = (
        near[0],
        lax.ppermute(near[1], "core", swap),
        lax.ppermute(near[2], "zl", swap),
        lax.ppermute(near[3], ("zl", "core"), [(i, 3 - i) for i in range(4)]),
    )
    _, near = lax.optimization_barrier((group, near))
    blocks = [jnp.stack([part[j] for part in near]) for j in range(4)]
    blocks = blocks[:1] + [lax.ppermute(blocks[j], "x", [(i, i ^ j) for i in range(4)]) for j in range(1, 4)]
    output, grad_in = call(place_kernel, [sds((nz, rows, cg, w), F32)] * 2, [index, *blocks], smem=1)

    padded = jnp.pad(group, ((0, ns - 27), (0, 0), (0, 0)))
    shares = swap_all(padded, SPACE)
    tap = shares.sum(0) * norm
    taps = swap_all(jnp.broadcast_to(tap[None], (ns, cg, ch)), SPACE)
    weight_grad = taps[:27].reshape(3, 3, 3, cg, ch).transpose(0, 1, 2, 4, 3)
    return output, grad_in, weight_grad


def solution(mesh):
    fine = Mesh(mesh.devices.reshape(8, 4, 2, 4, 2), SPACE + FILT)
    return jax.shard_map(
        step,
        mesh=fine,
        in_specs=(
            P(SPACE, None, FILT, None),
            P(None, None, None, None, FILT),
            P(SPACE, None, FILT, None),
        ),
        out_specs=(
            P(SPACE, None, FILT, None),
            P(SPACE, None, FILT, None),
            P(None, None, None, None, FILT),
        ),
        check_vma=False,
    )
```

```python
import jax
import jax.numpy as jnp
from jax import lax
from jax.experimental import pallas as pl
from jax.experimental.pallas import tpu as pltpu
from jax.sharding import Mesh
from jax.sharding import PartitionSpec as P


SPACE = ("y", "zh")
FILT = ("zl", "x", "core")
CHIPS = ("zl", "x")
BF, F32 = jnp.bfloat16, jnp.float32


def vmem_specs(n):
    return [pl.BlockSpec(memory_space=pltpu.VMEM)] * n


def call(kernel, outs, ins, scratch=(), smem=0, flops=0):
    specs = [pl.BlockSpec(memory_space=pltpu.SMEM)] * smem + vmem_specs(len(ins) - smem)
    moved = sum(a.size * a.dtype.itemsize for a in ins) + sum(o.size * o.dtype.itemsize for o in outs)
    return pl.pallas_call(
        kernel,
        out_shape=tuple(outs),
        in_specs=specs,
        out_specs=tuple(vmem_specs(len(outs))),
        scratch_shapes=list(scratch),
        cost_estimate=pl.CostEstimate(flops=flops, transcendentals=0, bytes_accessed=moved),
    )(*ins)


def place_of(index):
    return (index >> 3) & 1, (index >> 1) & 3, index & 1


def odd_slab(index):
    return (index >> 4) & 1 == 1


def pack_kernel(x_ref, g_ref, o_ref):
    n, _, nz, nr = o_ref.shape[:4]
    rows = x_ref.shape[1]
    zero = jnp.zeros(x_ref.shape[2:], x_ref.dtype)
    for k, ref in enumerate((x_ref, g_ref)):
        for z in range(nz):
            for d in range(n):
                for r in range(nr):
                    h = d * (nr - 2) + r - 1
                    o_ref[d, k, z, r] = ref[z, h] if 0 <= h < rows else zero


def halo_pick(index):
    odd = odd_slab(index)

    def pick(side, even, odd_side):
        even, odd_side = even.astype(F32), odd_side.astype(F32)
        return jnp.where(odd == (side == 0), even, odd_side).astype(BF)

    return pick


def pack_more_kernel(p_ref, w_ref, even_ref, odd_ref, o_ref):
    chips, total = o_ref.shape[:2]
    taps = w_ref.shape[0]
    rows = even_ref.shape[0]
    nr = (total - taps) // 2
    pick = halo_pick(p_ref[0])
    zero = jnp.zeros(w_ref.shape[1:], w_ref.dtype)
    for q in range(chips):
        for t in range(taps):
            o_ref[q, t] = w_ref[t]
        for p in range(2):
            for r in range(nr):
                h = q * (nr - 2) + r - 1
                o_ref[q, taps + p * nr + r] = pick(p, even_ref[h], odd_ref[h]) if 0 <= h < rows else zero


def shifted(value):
    lane = lax.broadcasted_iota(jnp.int32, value.shape, 1)
    w = value.shape[1]
    left = jnp.where(lane == 0, 0.0, pltpu.roll(value, 1, 1))
    right = jnp.where(lane == w - 1, 0.0, pltpu.roll(value, w - 1, 1))
    return left.astype(BF), value.astype(BF), right.astype(BF)


def stack(parts):
    return jnp.concatenate([p.astype(F32) for p in parts], 0)


def by_core(first, mine, other):
    parts = []
    for m, o in zip(mine, other):
        m, o = m.astype(F32), o.astype(F32)
        parts += [jnp.where(first, m, o), jnp.where(first, o, m)]
    return jnp.concatenate(parts, 0)


def build(planes, sizes, s_ref):
    nr, ch, w = sizes
    for p, plane in enumerate(planes):
        for r in range(nr):
            for c, v in enumerate(shifted(plane(r))):
                for h in range(nr - 2):
                    b = r - h
                    if 0 <= b < 3:
                        s_ref[p, pl.ds((3 * b + c) * ch, ch), pl.ds(h * w, w)] = v


def own_plane(own_ref, k, z):
    return lambda r: stack([own_ref[d, k, z, r] for d in range(own_ref.shape[0])])


def halo_plane(index, side, even_ref, odd_ref):
    take_even = odd_slab(index) == (side == 0)

    def rows(r):
        n = even_ref.shape[0]
        return jnp.where(take_even, stack([even_ref[d, r] for d in range(n)]), stack([odd_ref[d, r] for d in range(n)]))

    return rows


def x_planes(index, own_ref, even_ref, odd_ref):
    inner = [own_plane(own_ref, 0, z) for z in range(own_ref.shape[2])]
    return [halo_plane(index, 0, even_ref, odd_ref)] + inner + [halo_plane(index, 1, even_ref, odd_ref)]


def wgrad_kernel(p_ref, own_ref, even_ref, odd_ref, keep_ref, send_ref, s_ref, t_ref, o_ref, sems):
    n, _, nz, nr, cg, w = own_ref.shape
    nh, ch = nr - 2, n * cg
    build(x_planes(p_ref[0], own_ref, even_ref, odd_ref), (nr, ch, w), s_ref)
    for z in range(nz):
        for h in range(nh):
            t_ref[z, :, pl.ds(h * w, w)] = own_plane(own_ref, 1, z)(h + 1).astype(BF)
    core = place_of(p_ref[0])[2]
    for a in range(3):
        for b in range(3):
            total = None
            for z in range(nz):
                part = lax.dot_general(
                    t_ref[z],
                    s_ref[z + a, pl.ds(3 * b * ch, 3 * ch), :],
                    (((1,), (1,)), ((), ())),
                    preferred_element_type=F32,
                )
                total = part if total is None else total + part
            for c in range(3):
                for d in range(n):
                    slot = (d % 2) ^ core
                    o_ref[slot, d // 2, 9 * a + 3 * b + c] = total[d * cg : (d + 1) * cg, c * ch : (c + 1) * ch]
    copies = [
        pltpu.make_async_copy(o_ref.at[1], send_ref, sems.at[1]),
        pltpu.make_async_copy(o_ref.at[0], keep_ref, sems.at[0]),
    ]
    for copy in copies:
        copy.start()
    for copy in copies:
        copy.wait()


def conv_kernel(
    p_ref, own_ref, even_ref, odd_ref, mine_ref, other_ref, out0, out1, out2, out3, s_ref, wt_ref, wf_ref, o_ref, sems
):
    n, _, nz, nr, cg, w = own_ref.shape
    nh, ch = nr - 2, n * cg
    chips, total = mine_ref.shape[:2]
    taps = 27
    span = (total - taps) // 2
    zl, x, core = place_of(p_ref[0])
    first = core == 0
    for t in range(taps):
        a, bc = t // 9, t % 9
        block = by_core(first, [mine_ref[q, t] for q in range(chips)], [other_ref[q, t] for q in range(chips)])
        wt_ref[a, :, pl.ds(bc * ch, ch)] = block.astype(BF)
        wf_ref[2 - a, :, pl.ds((8 - bc) * ch, ch)] = block.T.astype(BF)

    def g_halo(p):
        def rows(r):
            i = taps + p * span + r + core * nh
            return by_core(first, [mine_ref[q, i] for q in range(chips)], [other_ref[q, i] for q in range(chips)])

        return rows

    g_planes = [g_halo(0)] + [own_plane(own_ref, 1, z) for z in range(nz)] + [g_halo(1)]
    build(x_planes(p_ref[0], own_ref, even_ref, odd_ref), (nr, ch, w), s_ref.at[0])
    build(g_planes, (nr, ch, w), s_ref.at[1])
    for k, w_ref in enumerate((wt_ref, wf_ref)):
        for z in range(nz):
            total = None
            for a in range(3):
                part = jnp.dot(w_ref[a], s_ref[k, z + a], preferred_element_type=F32)
                total = part if total is None else total + part
            for d in range(n):
                dzl, dx, dcore = place_of(d)
                slot = (2 * (dzl ^ zl) + (dcore ^ core), dx ^ x)
                for h in range(nh):
                    o_ref[(*slot, k, z, h)] = total[d * cg : (d + 1) * cg, h * w : (h + 1) * w]
    copies = [pltpu.make_async_copy(o_ref.at[j], ref, sems.at[j]) for j, ref in enumerate((out0, out1, out2, out3))]
    for copy in copies:
        copy.start()
    for copy in copies:
        copy.wait()


def place_kernel(p_ref, *refs):
    parts, outs = refs[:-2], refs[-2:]
    zl, x, core = place_of(p_ref[0])
    for dx, ref in enumerate(parts):
        for j in range(ref.shape[0]):
            source = ((zl ^ (j >> 1)) * 4 + (x ^ dx)) * 2 + (core ^ (j & 1))
            for k, o_ref in enumerate(outs):
                for z in range(ref.shape[2]):
                    for h in range(ref.shape[3]):
                        o_ref[z, source * ref.shape[3] + h] = ref[j, k, z, h]


def swap_all(array, axes):
    return lax.all_to_all(array, axes, 0, 0, tiled=True)


def step(activations, weight, grad_out):
    nz, rows, cg, w = activations.shape
    n = lax.axis_size(FILT)
    chips = lax.axis_size(CHIPS)
    ns = lax.axis_size(SPACE)
    ch = n * cg
    nr = rows // n + 2
    nh = nr - 2
    norm = float(nz * ns * rows * w) ** (-0.5)
    index = lax.axis_index(SPACE + FILT).astype(jnp.int32).reshape(1)
    parity = lax.axis_index(SPACE).astype(jnp.int32) & 1
    sides = [(nz - 1) * (1 - parity), (nz - 1) * parity]
    pairs = [[(i, i + 1) for i in range(first, ns - 1, 2)] for first in (0, 1)]
    pairs = [p + [(j, i) for i, j in p] for p in pairs]
    swap = [(0, 1), (1, 0)]
    sds = jax.ShapeDtypeStruct
    g_halos = [
        lax.ppermute(lax.dynamic_slice(grad_out, (side, 0, 0, 0), (1, rows, cg, w))[0], SPACE, pair)
        for side, pair in zip(sides, pairs)
    ]
    (packed,) = call(pack_kernel, [sds((n, 2, nz, nr, cg, w), BF)], [activations, grad_out])
    own = swap_all(packed, FILT)
    x_halos = [
        lax.ppermute(
            lax.dynamic_slice(own, (0, 0, side, 0, 0, 0), (n, 1, 1, nr, cg, w))[:, 0, 0], SPACE, pair
        )
        for side, pair in zip(sides, pairs)
    ]

    flat_w = weight.transpose(0, 1, 2, 4, 3).reshape(27, cg, ch)
    span = rows // chips + 2
    (more,) = call(pack_more_kernel, [sds((chips, 27 + 2 * span, cg, ch), BF)], [index, flat_w, *g_halos], smem=1)
    mine = swap_all(more, CHIPS)
    other = lax.ppermute(mine, "core", swap)

    any_spec = pl.BlockSpec(memory_space=pl.ANY)
    keep, send = pl.pallas_call(
        wgrad_kernel,
        out_shape=(sds((chips, 27, cg, ch), F32),) * 2,
        in_specs=[pl.BlockSpec(memory_space=pltpu.SMEM)] + vmem_specs(3),
        out_specs=(any_spec, any_spec),
        scratch_shapes=[
            pltpu.VMEM((nz + 2, 9 * ch, nh * w), BF),
            pltpu.VMEM((nz, ch, nh * w), BF),
            pltpu.VMEM((2, chips, 27, cg, ch), F32),
            pltpu.SemaphoreType.DMA((2,)),
        ],
        cost_estimate=pl.CostEstimate(
            flops=2 * 27 * ch * ch * nz * nh * w, transcendentals=0, bytes_accessed=4 * 27 * ch * ch
        ),
        name="wgrad",
    )(index, own, *x_halos)
    got = lax.ppermute(send, "core", swap)
    pair = keep + got
    pieces = swap_all(pair, CHIPS).reshape(chips, 27, cg, ch)
    group = pieces.sum(0)

    near = pl.pallas_call(
        conv_kernel,
        out_shape=(sds((4, 2, nz, nh, cg, w), F32),) * 4,
        in_specs=[pl.BlockSpec(memory_space=pltpu.SMEM)] + vmem_specs(5),
        out_specs=(any_spec,) * 4,
        scratch_shapes=[
            pltpu.VMEM((2, nz + 2, 9 * ch, nh * w), BF),
            pltpu.VMEM((3, ch, 9 * ch), BF),
            pltpu.VMEM((3, ch, 9 * ch), BF),
            pltpu.VMEM((4, 4, 2, nz, nh, cg, w), F32),
            pltpu.SemaphoreType.DMA((4,)),
        ],
        cost_estimate=pl.CostEstimate(
            flops=4 * 27 * ch * ch * nz * nh * w, transcendentals=0, bytes_accessed=4 * 27 * ch * ch
        ),
        name="conv",
    )(index, own, *x_halos, mine, other)
    near = (
        near[0],
        lax.ppermute(near[1], "core", swap),
        lax.ppermute(near[2], "zl", swap),
        lax.ppermute(near[3], ("zl", "core"), [(i, 3 - i) for i in range(4)]),
    )

    padded = jnp.pad(group, ((0, ns - 27), (0, 0), (0, 0)))
    shares = swap_all(padded, SPACE)
    _, near = lax.optimization_barrier((shares, near))
    tap = shares.sum(0) * norm
    taps = swap_all(jnp.broadcast_to(tap[None], (ns, cg, ch)), SPACE)
    blocks = {j: jnp.stack([part[j] for part in near]) for j in (2, 1, 3, 0)}
    blocks = {j: lax.ppermute(b, "x", [(i, i ^ j) for i in range(4)]) if j else b for j, b in blocks.items()}
    output, grad_in = call(
        place_kernel, [sds((nz, rows, cg, w), F32)] * 2, [index] + [blocks[j] for j in range(4)], smem=1
    )
    weight_grad = taps[:27].reshape(3, 3, 3, cg, ch).transpose(0, 1, 2, 4, 3)
    return output, grad_in, weight_grad


def solution(mesh):
    fine = Mesh(mesh.devices.reshape(8, 4, 2, 4, 2), SPACE + FILT)
    return jax.shard_map(
        step,
        mesh=fine,
        in_specs=(
            P(SPACE, None, FILT, None),
            P(None, None, None, None, FILT),
            P(SPACE, None, FILT, None),
        ),
        out_specs=(
            P(SPACE, None, FILT, None),
            P(SPACE, None, FILT, None),
            P(None, None, None, None, FILT),
        ),
        check_vma=False,
    )
```

```python
import functools
import math

import jax
import jax.numpy as jnp
from jax import lax
from jax.experimental import pallas as pl
from jax.experimental.pallas import tpu as pltpu
from jax.sharding import Mesh
from jax.sharding import PartitionSpec as P


SPACE = ("y", "zh")
FILT = ("zl", "x", "core")
CHIPS = ("zl", "x")
BF, F32 = jnp.bfloat16, jnp.float32


def vmem_specs(n):
    return [pl.BlockSpec(memory_space=pltpu.VMEM)] * n


def call(kernel, outs, ins, scratch=(), smem=0, flops=0):
    specs = [pl.BlockSpec(memory_space=pltpu.SMEM)] * smem + vmem_specs(len(ins) - smem)
    moved = sum(a.size * a.dtype.itemsize for a in ins) + sum(math.prod(o.shape) * 4 for o in outs)
    one = len(outs) == 1
    out_specs = vmem_specs(len(outs))
    result = pl.pallas_call(
        kernel,
        out_shape=outs[0] if one else tuple(outs),
        in_specs=specs,
        out_specs=out_specs[0] if one else tuple(out_specs),
        scratch_shapes=list(scratch),
        cost_estimate=pl.CostEstimate(flops=flops, transcendentals=0, bytes_accessed=moved),
    )(*ins)
    return (result,) if one else result


def near_core(array):
    return pltpu.with_memory_space_constraint(array, pltpu.VMEM)


def place_of(index):
    return (index >> 3) & 1, (index >> 1) & 3, index & 1


def odd_slab(index):
    return (index >> 4) & 1 == 1


def pack_kernel(x_ref, g_ref, o_ref):
    n, _, nz, nr = o_ref.shape[:4]
    rows = x_ref.shape[1]
    zero = jnp.zeros(x_ref.shape[2:], x_ref.dtype)
    for k, ref in enumerate((x_ref, g_ref)):
        for z in range(nz):
            for d in range(n):
                for r in range(nr):
                    h = d * (nr - 2) + r - 1
                    o_ref[d, k, z, r] = ref[z, h] if 0 <= h < rows else zero


def halo_pick(index):
    odd = odd_slab(index)

    def pick(side, even, odd_side):
        even, odd_side = even.astype(F32), odd_side.astype(F32)
        return jnp.where(odd == (side == 0), even, odd_side).astype(BF)

    return pick


def pack_more_kernel(p_ref, w_ref, even_ref, odd_ref, o_ref):
    chips, total = o_ref.shape[:2]
    taps = w_ref.shape[0]
    rows = even_ref.shape[0]
    nr = (total - taps) // 2
    pick = halo_pick(p_ref[0])
    zero = jnp.zeros(w_ref.shape[1:], w_ref.dtype)
    for q in range(chips):
        for t in range(taps):
            o_ref[q, t] = w_ref[t]
        for p in range(2):
            for r in range(nr):
                h = q * (nr - 2) + r - 1
                o_ref[q, taps + p * nr + r] = pick(p, even_ref[h], odd_ref[h]) if 0 <= h < rows else zero


def shifted(value):
    lane = lax.broadcasted_iota(jnp.int32, value.shape, 1)
    w = value.shape[1]
    left = jnp.where(lane == 0, 0.0, pltpu.roll(value, 1, 1))
    right = jnp.where(lane == w - 1, 0.0, pltpu.roll(value, w - 1, 1))
    return left.astype(BF), value.astype(BF), right.astype(BF)


def stack(parts):
    return jnp.concatenate([p.astype(F32) for p in parts], 0)


def by_core(first, mine, other):
    parts = []
    for m, o in zip(mine, other):
        m, o = m.astype(F32), o.astype(F32)
        parts += [jnp.where(first, m, o), jnp.where(first, o, m)]
    return jnp.concatenate(parts, 0)


def build(planes, sizes, s_ref):
    nr, ch, w = sizes
    for p, plane in enumerate(planes):
        for r in range(nr):
            for c, v in enumerate(shifted(plane(r))):
                for h in range(nr - 2):
                    b = r - h
                    if 0 <= b < 3:
                        s_ref[p, pl.ds((3 * b + c) * ch, ch), pl.ds(h * w, w)] = v


def own_plane(own_ref, k, z):
    return lambda r: stack([own_ref[d, k, z, r] for d in range(own_ref.shape[0])])


def halo_plane(index, side, even_ref, odd_ref):
    take_even = odd_slab(index) == (side == 0)

    def rows(r):
        n = even_ref.shape[0]
        return jnp.where(take_even, stack([even_ref[d, r] for d in range(n)]), stack([odd_ref[d, r] for d in range(n)]))

    return rows


def x_planes(index, own_ref, even_ref, odd_ref):
    inner = [own_plane(own_ref, 0, z) for z in range(own_ref.shape[2])]
    return [halo_plane(index, 0, even_ref, odd_ref)] + inner + [halo_plane(index, 1, even_ref, odd_ref)]


def wgrad_kernel(p_ref, own_ref, even_ref, odd_ref, keep_ref, send_ref, s_ref, t_ref):
    n, _, nz, nr, cg, w = own_ref.shape
    nh, ch = nr - 2, n * cg
    build(x_planes(p_ref[0], own_ref, even_ref, odd_ref), (nr, ch, w), s_ref)
    for z in range(nz):
        for h in range(nh):
            t_ref[z, :, pl.ds(h * w, w)] = own_plane(own_ref, 1, z)(h + 1).astype(BF)
    first = place_of(p_ref[0])[2] == 0
    for a in range(3):
        for b in range(3):
            total = None
            for z in range(nz):
                part = lax.dot_general(
                    t_ref[z],
                    s_ref[z + a, pl.ds(3 * b * ch, 3 * ch), :],
                    (((1,), (1,)), ((), ())),
                    preferred_element_type=F32,
                )
                total = part if total is None else total + part
            for c in range(3):
                tap = 9 * a + 3 * b + c
                for q in range(n // 2):
                    left, right = [
                        total[d * cg : (d + 1) * cg, c * ch : (c + 1) * ch] for d in (2 * q, 2 * q + 1)
                    ]
                    keep_ref[q, tap] = jnp.where(first, left, right)
                    send_ref[q, tap] = jnp.where(first, right, left)


def conv_kernel(
    p_ref, own_ref, even_ref, odd_ref, mine_ref, other_ref, out0, out1, out2, out3, s_ref, wt_ref, wf_ref
):
    n, _, nz, nr, cg, w = own_ref.shape
    nh, ch = nr - 2, n * cg
    chips, total = mine_ref.shape[:2]
    taps = 27
    span = (total - taps) // 2
    zl, x, core = place_of(p_ref[0])
    first = core == 0
    outs = (out0, out1, out2, out3)

    def targets(dx):
        return [[zl_to * 8 + dx * 2 + core_to for core_to in range(2)] for zl_to in range(2)]

    for t in range(taps):
        a, bc = t // 9, t % 9
        block = by_core(first, [mine_ref[q, t] for q in range(chips)], [other_ref[q, t] for q in range(chips)])
        wt_ref[a, :, pl.ds(bc * ch, ch)] = block.astype(BF)
        wf_ref[2 - a, :, pl.ds((8 - bc) * ch, ch)] = block.T.astype(BF)

    def g_halo(p):
        def rows(r):
            i = taps + p * span + r + core * nh
            return by_core(first, [mine_ref[q, i] for q in range(chips)], [other_ref[q, i] for q in range(chips)])

        return rows

    g_planes = [g_halo(0)] + [own_plane(own_ref, 1, z) for z in range(nz)] + [g_halo(1)]
    build(x_planes(p_ref[0], own_ref, even_ref, odd_ref), (nr, ch, w), s_ref.at[0])
    build(g_planes, (nr, ch, w), s_ref.at[1])
    for k, w_ref in enumerate((wt_ref, wf_ref)):
        for z in range(nz):
            total = None
            for a in range(3):
                part = jnp.dot(w_ref[a], s_ref[k, z + a], preferred_element_type=F32)
                total = part if total is None else total + part
            for dx in range(4):
                for h in range(nh):
                    tiles = [[total[d * cg : (d + 1) * cg, h * w : (h + 1) * w] for d in pair] for pair in targets(dx)]
                    tiles = [
                        [jnp.where(core == 0, t[0], t[1]), jnp.where(core == 0, t[1], t[0])] for t in tiles
                    ]
                    for j in range(2):
                        low = jnp.where(zl == 0, tiles[0][j], tiles[1][j])
                        high = jnp.where(zl == 0, tiles[1][j], tiles[0][j])
                        outs[j][dx ^ x, k, z, h] = low
                        outs[2 + j][dx ^ x, k, z, h] = high


def chips_add_kernel(pieces_ref, o_ref):
    taps = pieces_ref.shape[1]
    for t in range(o_ref.shape[0]):
        if t < taps:
            total = pieces_ref[0, t]
            for q in range(1, pieces_ref.shape[0]):
                total = total + pieces_ref[q, t]
        else:
            total = jnp.zeros(o_ref.shape[1:], F32)
        o_ref[t] = total


def space_add_kernel(shares_ref, o_ref, *, norm):
    total = shares_ref[0]
    for j in range(1, shares_ref.shape[0]):
        total = total + shares_ref[j]
    total = total * norm
    for j in range(o_ref.shape[0]):
        o_ref[j] = total


def place_kernel(p_ref, *refs):
    parts, outs = refs[:-2], refs[-2:]
    zl, x, core = place_of(p_ref[0])
    for dx, ref in enumerate(parts):
        for j in range(ref.shape[0]):
            source = ((zl ^ (j >> 1)) * 4 + (x ^ dx)) * 2 + (core ^ (j & 1))
            for k, o_ref in enumerate(outs):
                for z in range(ref.shape[2]):
                    for h in range(ref.shape[3]):
                        o_ref[z, source * ref.shape[3] + h] = ref[j, k, z, h]


def swap_all(array, axes):
    return lax.all_to_all(array, axes, 0, 0, tiled=True)


def step(activations, weight, grad_out):
    nz, rows, cg, w = activations.shape
    n = lax.axis_size(FILT)
    chips = lax.axis_size(CHIPS)
    ns = lax.axis_size(SPACE)
    ch = n * cg
    nr = rows // n + 2
    nh = nr - 2
    norm = float(nz * ns * rows * w) ** (-0.5)
    index = lax.axis_index(SPACE + FILT).astype(jnp.int32).reshape(1)
    parity = lax.axis_index(SPACE).astype(jnp.int32) & 1
    sides = [(nz - 1) * (1 - parity), (nz - 1) * parity]
    pairs = [[(i, i + 1) for i in range(first, ns - 1, 2)] for first in (0, 1)]
    pairs = [p + [(j, i) for i, j in p] for p in pairs]
    swap = [(0, 1), (1, 0)]
    sds = jax.ShapeDtypeStruct
    g_halos = [
        lax.ppermute(lax.dynamic_slice(grad_out, (side, 0, 0, 0), (1, rows, cg, w))[0], SPACE, pair)
        for side, pair in zip(sides, pairs)
    ]
    (packed,) = call(pack_kernel, [pltpu.VMEM((n, 2, nz, nr, cg, w), BF)], [activations, grad_out])
    own = swap_all(packed, FILT)
    x_halos = [
        lax.ppermute(
            lax.dynamic_slice(own, (0, 0, side, 0, 0, 0), (n, 1, 1, nr, cg, w))[:, 0, 0], SPACE, pair
        )
        for side, pair in zip(sides, pairs)
    ]
    local = [index, near_core(own), *map(near_core, x_halos)]

    flat_w = weight.transpose(0, 1, 2, 4, 3).reshape(27, cg, ch)
    span = rows // chips + 2
    (more,) = call(pack_more_kernel, [sds((chips, 27 + 2 * span, cg, ch), BF)], [index, flat_w, *map(near_core, g_halos)], smem=1)
    mine = swap_all(more, CHIPS)
    other = lax.ppermute(mine, "core", swap)

    keep, send = call(
        wgrad_kernel,
        [pltpu.VMEM((chips, 27, cg, ch), F32)] * 2,
        local,
        scratch=[pltpu.VMEM((nz + 2, 9 * ch, nh * w), BF), pltpu.VMEM((nz, ch, nh * w), BF)],
        smem=1,
        flops=2 * 27 * ch * ch * nz * nh * w,
    )
    got = lax.ppermute(send, "core", swap)
    pair = keep + got
    pieces = swap_all(pair, CHIPS).reshape(chips, 27, cg, ch)
    (padded,) = call(chips_add_kernel, [pltpu.VMEM((ns, cg, ch), F32)], [near_core(pieces)])

    near = call(
        conv_kernel,
        [pltpu.VMEM((4, 2, nz, nh, cg, w), F32)] * 4,
        local + [mine, other],
        scratch=[pltpu.VMEM((2, nz + 2, 9 * ch, nh * w), BF)] + [pltpu.VMEM((3, ch, 9 * ch), BF)] * 2,
        smem=1,
        flops=4 * 27 * ch * ch * nz * nh * w,
    )
    near = (
        near[0],
        lax.ppermute(near[1], "core", swap),
        lax.ppermute(near[2], "zl", swap),
        lax.ppermute(near[3], ("zl", "core"), [(i, 3 - i) for i in range(4)]),
    )
    shares = swap_all(padded, SPACE)
    _, near = lax.optimization_barrier((shares, near))
    (tap,) = call(functools.partial(space_add_kernel, norm=norm), [pltpu.VMEM((ns, cg, ch), F32)], [near_core(shares)])
    taps = swap_all(tap, SPACE)
    blocks = {j: jnp.stack([part[j] for part in near]) for j in (2, 1, 3, 0)}
    blocks = {j: lax.ppermute(b, "x", [(i, i ^ j) for i in range(4)]) if j else b for j, b in blocks.items()}
    output, grad_in = call(
        place_kernel, [sds((nz, rows, cg, w), F32)] * 2, [index] + [near_core(blocks[j]) for j in range(4)], smem=1
    )
    weight_grad = taps[:27].reshape(3, 3, 3, cg, ch).transpose(0, 1, 2, 4, 3)
    return output, grad_in, weight_grad


def solution(mesh):
    fine = Mesh(mesh.devices.reshape(8, 4, 2, 4, 2), SPACE + FILT)
    return jax.shard_map(
        step,
        mesh=fine,
        in_specs=(
            P(SPACE, None, FILT, None),
            P(None, None, None, None, FILT),
            P(SPACE, None, FILT, None),
        ),
        out_specs=(
            P(SPACE, None, FILT, None),
            P(SPACE, None, FILT, None),
            P(None, None, None, None, FILT),
        ),
        check_vma=False,
    )
```

```python
import functools
import math

import jax
import jax.numpy as jnp
from jax import lax
from jax.experimental import pallas as pl
from jax.experimental.pallas import tpu as pltpu
from jax.sharding import Mesh
from jax.sharding import PartitionSpec as P


SPACE = ("y", "zh")
FILT = ("zl", "x", "core")
CHIPS = ("zl", "x")
BF, F32 = jnp.bfloat16, jnp.float32


def vmem_specs(n):
    return [pl.BlockSpec(memory_space=pltpu.VMEM)] * n


def call(kernel, outs, ins, scratch=(), smem=0, flops=0):
    specs = [pl.BlockSpec(memory_space=pltpu.SMEM)] * smem + vmem_specs(len(ins) - smem)
    moved = sum(a.size * a.dtype.itemsize for a in ins) + sum(math.prod(o.shape) * 4 for o in outs)
    one = len(outs) == 1
    out_specs = vmem_specs(len(outs))
    result = pl.pallas_call(
        kernel,
        out_shape=outs[0] if one else tuple(outs),
        in_specs=specs,
        out_specs=out_specs[0] if one else tuple(out_specs),
        scratch_shapes=list(scratch),
        cost_estimate=pl.CostEstimate(flops=flops, transcendentals=0, bytes_accessed=moved),
    )(*ins)
    return (result,) if one else result


def near_core(array):
    return pltpu.with_memory_space_constraint(array, pltpu.VMEM)


def place_of(index):
    return (index >> 3) & 1, (index >> 1) & 3, index & 1


def odd_slab(index):
    return (index >> 4) & 1 == 1


def pack_kernel(x_ref, g_ref, o_ref):
    n, _, nz, nr = o_ref.shape[:4]
    rows = x_ref.shape[1]
    zero = jnp.zeros(x_ref.shape[2:], x_ref.dtype)
    for k, ref in enumerate((x_ref, g_ref)):
        for z in range(nz):
            for d in range(n):
                for r in range(nr):
                    h = d * (nr - 2) + r - 1
                    o_ref[d, k, z, r] = ref[z, h] if 0 <= h < rows else zero


def halo_pick(index):
    odd = odd_slab(index)

    def pick(side, even, odd_side):
        even, odd_side = even.astype(F32), odd_side.astype(F32)
        return jnp.where(odd == (side == 0), even, odd_side).astype(BF)

    return pick


def pack_more_kernel(p_ref, w_ref, even_ref, odd_ref, o_ref):
    chips, total = o_ref.shape[:2]
    taps = w_ref.shape[0]
    rows = even_ref.shape[0]
    nr = (total - taps) // 2
    pick = halo_pick(p_ref[0])
    zero = jnp.zeros(w_ref.shape[1:], w_ref.dtype)
    for q in range(chips):
        for t in range(taps):
            o_ref[q, t] = w_ref[t]
        for p in range(2):
            for r in range(nr):
                h = q * (nr - 2) + r - 1
                o_ref[q, taps + p * nr + r] = pick(p, even_ref[h], odd_ref[h]) if 0 <= h < rows else zero


def shifted(value):
    lane = lax.broadcasted_iota(jnp.int32, value.shape, 1)
    w = value.shape[1]
    left = jnp.where(lane == 0, 0.0, pltpu.roll(value, 1, 1))
    right = jnp.where(lane == w - 1, 0.0, pltpu.roll(value, w - 1, 1))
    return left.astype(BF), value.astype(BF), right.astype(BF)


def stack(parts):
    return jnp.concatenate([p.astype(F32) for p in parts], 0)


def by_core(first, mine, other):
    parts = []
    for m, o in zip(mine, other):
        m, o = m.astype(F32), o.astype(F32)
        parts += [jnp.where(first, m, o), jnp.where(first, o, m)]
    return jnp.concatenate(parts, 0)


def build(planes, sizes, s_ref):
    nr, ch, w = sizes
    for p, plane in enumerate(planes):
        for r in range(nr):
            for c, v in enumerate(shifted(plane(r))):
                for h in range(nr - 2):
                    b = r - h
                    if 0 <= b < 3:
                        s_ref[p, pl.ds((3 * b + c) * ch, ch), pl.ds(h * w, w)] = v


def own_plane(own_ref, k, z):
    return lambda r: stack([own_ref[d, k, z, r] for d in range(own_ref.shape[0])])


def halo_plane(index, side, even_ref, odd_ref):
    take_even = odd_slab(index) == (side == 0)

    def rows(r):
        n = even_ref.shape[0]
        return jnp.where(take_even, stack([even_ref[d, r] for d in range(n)]), stack([odd_ref[d, r] for d in range(n)]))

    return rows


def x_planes(index, own_ref, even_ref, odd_ref):
    inner = [own_plane(own_ref, 0, z) for z in range(own_ref.shape[2])]
    return [halo_plane(index, 0, even_ref, odd_ref)] + inner + [halo_plane(index, 1, even_ref, odd_ref)]


def wgrad_kernel(p_ref, own_ref, even_ref, odd_ref, keep_ref, send_ref, s_ref, t_ref):
    n, _, nz, nr, cg, w = own_ref.shape
    nh, ch = nr - 2, n * cg
    build(x_planes(p_ref[0], own_ref, even_ref, odd_ref), (nr, ch, w), s_ref)
    for z in range(nz):
        for h in range(nh):
            t_ref[z, :, pl.ds(h * w, w)] = own_plane(own_ref, 1, z)(h + 1).astype(BF)
    first = place_of(p_ref[0])[2] == 0
    for a in range(3):
        for b in range(3):
            total = None
            for z in range(nz):
                part = lax.dot_general(
                    t_ref[z],
                    s_ref[z + a, pl.ds(3 * b * ch, 3 * ch), :],
                    (((1,), (1,)), ((), ())),
                    preferred_element_type=F32,
                )
                total = part if total is None else total + part
            for c in range(3):
                tap = 9 * a + 3 * b + c
                for q in range(n // 2):
                    left, right = [
                        total[d * cg : (d + 1) * cg, c * ch : (c + 1) * ch] for d in (2 * q, 2 * q + 1)
                    ]
                    keep_ref[q, tap] = jnp.where(first, left, right)
                    send_ref[q, tap] = jnp.where(first, right, left)


def pair_add_kernel(keep_ref, got_ref, o_ref, sum_ref, sems):
    count = keep_ref.shape[0]
    stores = [pltpu.make_async_copy(sum_ref.at[q], o_ref.at[q], sems.at[q]) for q in range(count)]
    for q in range(count):
        sum_ref[q] = keep_ref[q] + got_ref[q]
        stores[q].start()
    for store in stores:
        store.wait()


def conv_kernel(
    p_ref, own_ref, even_ref, odd_ref, mine_ref, other_ref, out0, out1, out2, out3, s_ref, wt_ref, wf_ref
):
    n, _, nz, nr, cg, w = own_ref.shape
    nh, ch = nr - 2, n * cg
    chips, total = mine_ref.shape[:2]
    taps = 27
    span = (total - taps) // 2
    zl, x, core = place_of(p_ref[0])
    first = core == 0
    outs = (out0, out1, out2, out3)

    def targets(dx):
        return [[zl_to * 8 + dx * 2 + core_to for core_to in range(2)] for zl_to in range(2)]

    for t in range(taps):
        a, bc = t // 9, t % 9
        block = by_core(first, [mine_ref[q, t] for q in range(chips)], [other_ref[q, t] for q in range(chips)])
        wt_ref[a, :, pl.ds(bc * ch, ch)] = block.astype(BF)
        wf_ref[2 - a, :, pl.ds((8 - bc) * ch, ch)] = block.T.astype(BF)

    def g_halo(p):
        def rows(r):
            i = taps + p * span + r + core * nh
            return by_core(first, [mine_ref[q, i] for q in range(chips)], [other_ref[q, i] for q in range(chips)])

        return rows

    g_planes = [g_halo(0)] + [own_plane(own_ref, 1, z) for z in range(nz)] + [g_halo(1)]
    build(x_planes(p_ref[0], own_ref, even_ref, odd_ref), (nr, ch, w), s_ref.at[0])
    build(g_planes, (nr, ch, w), s_ref.at[1])
    for k, w_ref in enumerate((wt_ref, wf_ref)):
        for z in range(nz):
            total = None
            for a in range(3):
                part = jnp.dot(w_ref[a], s_ref[k, z + a], preferred_element_type=F32)
                total = part if total is None else total + part
            for dx in range(4):
                for h in range(nh):
                    tiles = [[total[d * cg : (d + 1) * cg, h * w : (h + 1) * w] for d in pair] for pair in targets(dx)]
                    tiles = [
                        [jnp.where(core == 0, t[0], t[1]), jnp.where(core == 0, t[1], t[0])] for t in tiles
                    ]
                    for j in range(2):
                        low = jnp.where(zl == 0, tiles[0][j], tiles[1][j])
                        high = jnp.where(zl == 0, tiles[1][j], tiles[0][j])
                        outs[j][dx ^ x, k, z, h] = low
                        outs[2 + j][dx ^ x, k, z, h] = high


def chips_add_kernel(pieces_ref, o_ref):
    taps = pieces_ref.shape[1]
    for t in range(o_ref.shape[0]):
        if t < taps:
            total = pieces_ref[0, t]
            for q in range(1, pieces_ref.shape[0]):
                total = total + pieces_ref[q, t]
        else:
            total = jnp.zeros(o_ref.shape[1:], F32)
        o_ref[t] = total


def space_add_kernel(shares_ref, o_ref, *, norm):
    total = shares_ref[0]
    for j in range(1, shares_ref.shape[0]):
        total = total + shares_ref[j]
    total = total * norm
    for j in range(o_ref.shape[0]):
        o_ref[j] = total


def place_kernel(p_ref, *refs):
    parts, outs = refs[:-2], refs[-2:]
    zl, x, core = place_of(p_ref[0])
    for dx, ref in enumerate(parts):
        for j in range(ref.shape[0]):
            source = ((zl ^ (j >> 1)) * 4 + (x ^ dx)) * 2 + (core ^ (j & 1))
            for k, o_ref in enumerate(outs):
                for z in range(ref.shape[2]):
                    for h in range(ref.shape[3]):
                        o_ref[z, source * ref.shape[3] + h] = ref[j, k, z, h]


def swap_all(array, axes):
    return lax.all_to_all(array, axes, 0, 0, tiled=True)


def step(activations, weight, grad_out):
    nz, rows, cg, w = activations.shape
    n = lax.axis_size(FILT)
    chips = lax.axis_size(CHIPS)
    ns = lax.axis_size(SPACE)
    ch = n * cg
    nr = rows // n + 2
    nh = nr - 2
    norm = float(nz * ns * rows * w) ** (-0.5)
    index = lax.axis_index(SPACE + FILT).astype(jnp.int32).reshape(1)
    parity = lax.axis_index(SPACE).astype(jnp.int32) & 1
    sides = [(nz - 1) * (1 - parity), (nz - 1) * parity]
    pairs = [[(i, i + 1) for i in range(first, ns - 1, 2)] for first in (0, 1)]
    pairs = [p + [(j, i) for i, j in p] for p in pairs]
    swap = [(0, 1), (1, 0)]
    sds = jax.ShapeDtypeStruct
    g_halos = [
        lax.ppermute(lax.dynamic_slice(grad_out, (side, 0, 0, 0), (1, rows, cg, w))[0], SPACE, pair)
        for side, pair in zip(sides, pairs)
    ]
    (packed,) = call(pack_kernel, [pltpu.VMEM((n, 2, nz, nr, cg, w), BF)], [activations, grad_out])
    own = swap_all(packed, FILT)
    x_halos = [
        lax.ppermute(
            lax.dynamic_slice(own, (0, 0, side, 0, 0, 0), (n, 1, 1, nr, cg, w))[:, 0, 0], SPACE, pair
        )
        for side, pair in zip(sides, pairs)
    ]
    local = [index, near_core(own), *map(near_core, x_halos)]

    flat_w = weight.transpose(0, 1, 2, 4, 3).reshape(27, cg, ch)
    span = rows // chips + 2
    (more,) = call(pack_more_kernel, [sds((chips, 27 + 2 * span, cg, ch), BF)], [index, flat_w, *map(near_core, g_halos)], smem=1)
    mine = swap_all(more, CHIPS)
    other = lax.ppermute(mine, "core", swap)

    keep, send = call(
        wgrad_kernel,
        [pltpu.VMEM((chips, 27, cg, ch), F32)] * 2,
        local,
        scratch=[pltpu.VMEM((nz + 2, 9 * ch, nh * w), BF), pltpu.VMEM((nz, ch, nh * w), BF)],
        smem=1,
        flops=2 * 27 * ch * ch * nz * nh * w,
    )
    got = lax.ppermute(send, "core", swap)
    pair = pl.pallas_call(
        pair_add_kernel,
        out_shape=sds((chips, 27, cg, ch), F32),
        in_specs=vmem_specs(2),
        out_specs=pl.BlockSpec(memory_space=pl.ANY),
        scratch_shapes=[pltpu.VMEM((chips, 27, cg, ch), F32), pltpu.SemaphoreType.DMA((chips,))],
        name="pair_add",
    )(near_core(keep), near_core(got))
    pieces = swap_all(pair, CHIPS).reshape(chips, 27, cg, ch)
    (padded,) = call(chips_add_kernel, [pltpu.VMEM((ns, cg, ch), F32)], [near_core(pieces)])

    near = call(
        conv_kernel,
        [pltpu.VMEM((4, 2, nz, nh, cg, w), F32)] * 4,
        local + [mine, other],
        scratch=[pltpu.VMEM((2, nz + 2, 9 * ch, nh * w), BF)] + [pltpu.VMEM((3, ch, 9 * ch), BF)] * 2,
        smem=1,
        flops=4 * 27 * ch * ch * nz * nh * w,
    )
    near = (
        near[0],
        lax.ppermute(near[1], "core", swap),
        lax.ppermute(near[2], "zl", swap),
        lax.ppermute(near[3], ("zl", "core"), [(i, 3 - i) for i in range(4)]),
    )
    shares = swap_all(padded, SPACE)
    _, near = lax.optimization_barrier((padded, near))
    (tap,) = call(functools.partial(space_add_kernel, norm=norm), [pltpu.VMEM((ns, cg, ch), F32)], [near_core(shares)])
    taps = swap_all(tap, SPACE)
    blocks = {j: jnp.stack([part[j] for part in near]) for j in range(4)}
    for j in (2, 1, 3):
        blocks[j] = lax.ppermute(blocks[j], "x", [(i, i ^ j) for i in range(4)])
    output, grad_in = call(
        place_kernel, [sds((nz, rows, cg, w), F32)] * 2, [index] + [near_core(blocks[j]) for j in range(4)], smem=1
    )
    weight_grad = taps[:27].reshape(3, 3, 3, cg, ch).transpose(0, 1, 2, 4, 3)
    return output, grad_in, weight_grad


def solution(mesh):
    fine = Mesh(mesh.devices.reshape(8, 4, 2, 4, 2), SPACE + FILT)
    return jax.shard_map(
        step,
        mesh=fine,
        in_specs=(
            P(SPACE, None, FILT, None),
            P(None, None, None, None, FILT),
            P(SPACE, None, FILT, None),
        ),
        out_specs=(
            P(SPACE, None, FILT, None),
            P(SPACE, None, FILT, None),
            P(None, None, None, None, FILT),
        ),
        check_vma=False,
    )
```

```python
import functools
import math

import jax
import jax.numpy as jnp
from jax import lax
from jax.experimental import pallas as pl
from jax.experimental.pallas import tpu as pltpu
from jax.sharding import Mesh
from jax.sharding import PartitionSpec as P


SPACE = ("y", "zh")
FILT = ("zl", "x", "core")
CHIPS = ("zl", "x")
BF, F32 = jnp.bfloat16, jnp.float32


def vmem_specs(n):
    return [pl.BlockSpec(memory_space=pltpu.VMEM)] * n


def call(kernel, outs, ins, scratch=(), smem=0, flops=0):
    specs = [pl.BlockSpec(memory_space=pltpu.SMEM)] * smem + vmem_specs(len(ins) - smem)
    moved = sum(a.size * a.dtype.itemsize for a in ins) + sum(math.prod(o.shape) * 4 for o in outs)
    one = len(outs) == 1
    out_specs = vmem_specs(len(outs))
    result = pl.pallas_call(
        kernel,
        out_shape=outs[0] if one else tuple(outs),
        in_specs=specs,
        out_specs=out_specs[0] if one else tuple(out_specs),
        scratch_shapes=list(scratch),
        cost_estimate=pl.CostEstimate(flops=flops, transcendentals=0, bytes_accessed=moved),
    )(*ins)
    return (result,) if one else result


def near_core(array):
    return pltpu.with_memory_space_constraint(array, pltpu.VMEM)


def place_of(index):
    return (index >> 3) & 1, (index >> 1) & 3, index & 1


def odd_slab(index):
    return (index >> 4) & 1 == 1


def pack_kernel(x_ref, g_ref, o_ref):
    n, _, nz, nr = o_ref.shape[:4]
    rows = x_ref.shape[1]
    zero = jnp.zeros(x_ref.shape[2:], x_ref.dtype)
    for k, ref in enumerate((x_ref, g_ref)):
        for z in range(nz):
            for d in range(n):
                for r in range(nr):
                    h = d * (nr - 2) + r - 1
                    o_ref[d, k, z, r] = ref[z, h] if 0 <= h < rows else zero


def halo_pick(index):
    odd = odd_slab(index)

    def pick(side, even, odd_side):
        even, odd_side = even.astype(F32), odd_side.astype(F32)
        return jnp.where(odd == (side == 0), even, odd_side).astype(BF)

    return pick


def pack_more_kernel(p_ref, w_ref, even_ref, odd_ref, o_ref):
    chips, total = o_ref.shape[:2]
    taps = w_ref.shape[0]
    rows = even_ref.shape[0]
    nr = (total - taps) // 2
    pick = halo_pick(p_ref[0])
    zero = jnp.zeros(w_ref.shape[1:], w_ref.dtype)
    for q in range(chips):
        for t in range(taps):
            o_ref[q, t] = w_ref[t]
        for p in range(2):
            for r in range(nr):
                h = q * (nr - 2) + r - 1
                o_ref[q, taps + p * nr + r] = pick(p, even_ref[h], odd_ref[h]) if 0 <= h < rows else zero


def shifted(value):
    lane = lax.broadcasted_iota(jnp.int32, value.shape, 1)
    w = value.shape[1]
    left = jnp.where(lane == 0, 0.0, pltpu.roll(value, 1, 1))
    right = jnp.where(lane == w - 1, 0.0, pltpu.roll(value, w - 1, 1))
    return left.astype(BF), value.astype(BF), right.astype(BF)


def stack(parts):
    return jnp.concatenate([p.astype(F32) for p in parts], 0)


def by_core(first, mine, other):
    parts = []
    for m, o in zip(mine, other):
        m, o = m.astype(F32), o.astype(F32)
        parts += [jnp.where(first, m, o), jnp.where(first, o, m)]
    return jnp.concatenate(parts, 0)


def build(planes, sizes, s_ref):
    nr, ch, w = sizes
    for p, plane in enumerate(planes):
        for r in range(nr):
            for c, v in enumerate(shifted(plane(r))):
                for h in range(nr - 2):
                    b = r - h
                    if 0 <= b < 3:
                        s_ref[p, pl.ds((3 * b + c) * ch, ch), pl.ds(h * w, w)] = v


def own_plane(own_ref, k, z):
    return lambda r: stack([own_ref[d, k, z, r] for d in range(own_ref.shape[0])])


def halo_plane(index, side, even_ref, odd_ref):
    take_even = odd_slab(index) == (side == 0)

    def rows(r):
        n = even_ref.shape[0]
        return jnp.where(take_even, stack([even_ref[d, r] for d in range(n)]), stack([odd_ref[d, r] for d in range(n)]))

    return rows


def x_planes(index, own_ref, even_ref, odd_ref):
    inner = [own_plane(own_ref, 0, z) for z in range(own_ref.shape[2])]
    return [halo_plane(index, 0, even_ref, odd_ref)] + inner + [halo_plane(index, 1, even_ref, odd_ref)]


def wgrad_kernel(p_ref, own_ref, even_ref, odd_ref, keep_ref, send_ref, s_ref, t_ref):
    n, _, nz, nr, cg, w = own_ref.shape
    nh, ch = nr - 2, n * cg
    build(x_planes(p_ref[0], own_ref, even_ref, odd_ref), (nr, ch, w), s_ref)
    for z in range(nz):
        for h in range(nh):
            t_ref[z, :, pl.ds(h * w, w)] = own_plane(own_ref, 1, z)(h + 1).astype(BF)
    first = place_of(p_ref[0])[2] == 0
    for a in range(3):
        for b in range(3):
            total = None
            for z in range(nz):
                part = lax.dot_general(
                    t_ref[z],
                    s_ref[z + a, pl.ds(3 * b * ch, 3 * ch), :],
                    (((1,), (1,)), ((), ())),
                    preferred_element_type=F32,
                )
                total = part if total is None else total + part
            for c in range(3):
                tap = 9 * a + 3 * b + c
                for q in range(n // 2):
                    left, right = [
                        total[d * cg : (d + 1) * cg, c * ch : (c + 1) * ch] for d in (2 * q, 2 * q + 1)
                    ]
                    keep_ref[q, tap] = jnp.where(first, left, right)
                    send_ref[q, tap] = jnp.where(first, right, left)


def conv_kernel(
    p_ref, own_ref, even_ref, odd_ref, mine_ref, other_ref, out0, out1, out2, out3, s_ref, wt_ref, wf_ref
):
    n, _, nz, nr, cg, w = own_ref.shape
    nh, ch = nr - 2, n * cg
    chips, total = mine_ref.shape[:2]
    taps = 27
    span = (total - taps) // 2
    zl, x, core = place_of(p_ref[0])
    first = core == 0
    outs = (out0, out1, out2, out3)

    def targets(dx):
        return [[zl_to * 8 + dx * 2 + core_to for core_to in range(2)] for zl_to in range(2)]

    for t in range(taps):
        a, bc = t // 9, t % 9
        block = by_core(first, [mine_ref[q, t] for q in range(chips)], [other_ref[q, t] for q in range(chips)])
        wt_ref[a, :, pl.ds(bc * ch, ch)] = block.astype(BF)
        wf_ref[2 - a, :, pl.ds((8 - bc) * ch, ch)] = block.T.astype(BF)

    def g_halo(p):
        def rows(r):
            i = taps + p * span + r + core * nh
            return by_core(first, [mine_ref[q, i] for q in range(chips)], [other_ref[q, i] for q in range(chips)])

        return rows

    g_planes = [g_halo(0)] + [own_plane(own_ref, 1, z) for z in range(nz)] + [g_halo(1)]
    build(x_planes(p_ref[0], own_ref, even_ref, odd_ref), (nr, ch, w), s_ref.at[0])
    build(g_planes, (nr, ch, w), s_ref.at[1])
    for k, w_ref in enumerate((wt_ref, wf_ref)):
        for z in range(nz):
            total = None
            for a in range(3):
                part = jnp.dot(w_ref[a], s_ref[k, z + a], preferred_element_type=F32)
                total = part if total is None else total + part
            for dx in range(4):
                for h in range(nh):
                    tiles = [[total[d * cg : (d + 1) * cg, h * w : (h + 1) * w] for d in pair] for pair in targets(dx)]
                    tiles = [
                        [jnp.where(core == 0, t[0], t[1]), jnp.where(core == 0, t[1], t[0])] for t in tiles
                    ]
                    for j in range(2):
                        low = jnp.where(zl == 0, tiles[0][j], tiles[1][j])
                        high = jnp.where(zl == 0, tiles[1][j], tiles[0][j])
                        outs[j][dx ^ x, k, z, h] = low
                        outs[2 + j][dx ^ x, k, z, h] = high


def chips_add_kernel(pieces_ref, o_ref):
    taps = pieces_ref.shape[1]
    for t in range(o_ref.shape[0]):
        if t < taps:
            total = pieces_ref[0, t]
            for q in range(1, pieces_ref.shape[0]):
                total = total + pieces_ref[q, t]
        else:
            total = jnp.zeros(o_ref.shape[1:], F32)
        o_ref[t] = total


def space_add_kernel(shares_ref, o_ref, *, norm):
    total = shares_ref[0]
    for j in range(1, shares_ref.shape[0]):
        total = total + shares_ref[j]
    total = total * norm
    for j in range(o_ref.shape[0]):
        o_ref[j] = total


def place_kernel(p_ref, *refs):
    parts, outs = refs[:-2], refs[-2:]
    zl, x, core = place_of(p_ref[0])
    for dx, ref in enumerate(parts):
        for j in range(ref.shape[0]):
            source = ((zl ^ (j >> 1)) * 4 + (x ^ dx)) * 2 + (core ^ (j & 1))
            for k, o_ref in enumerate(outs):
                for z in range(ref.shape[2]):
                    for h in range(ref.shape[3]):
                        o_ref[z, source * ref.shape[3] + h] = ref[j, k, z, h]


def swap_all(array, axes):
    return lax.all_to_all(array, axes, 0, 0, tiled=True)


def step(activations, weight, grad_out):
    nz, rows, cg, w = activations.shape
    n = lax.axis_size(FILT)
    chips = lax.axis_size(CHIPS)
    ns = lax.axis_size(SPACE)
    ch = n * cg
    nr = rows // n + 2
    nh = nr - 2
    norm = float(nz * ns * rows * w) ** (-0.5)
    index = lax.axis_index(SPACE + FILT).astype(jnp.int32).reshape(1)
    parity = lax.axis_index(SPACE).astype(jnp.int32) & 1
    sides = [(nz - 1) * (1 - parity), (nz - 1) * parity]
    pairs = [[(i, i + 1) for i in range(first, ns - 1, 2)] for first in (0, 1)]
    pairs = [p + [(j, i) for i, j in p] for p in pairs]
    swap = [(0, 1), (1, 0)]
    sds = jax.ShapeDtypeStruct
    g_halos = [
        lax.ppermute(lax.dynamic_slice(grad_out, (side, 0, 0, 0), (1, rows, cg, w))[0], SPACE, pair)
        for side, pair in zip(sides, pairs)
    ]
    (packed,) = call(pack_kernel, [pltpu.VMEM((n, 2, nz, nr, cg, w), BF)], [activations, grad_out])
    own = swap_all(packed, FILT)
    x_halos = [
        lax.ppermute(
            lax.dynamic_slice(own, (0, 0, side, 0, 0, 0), (n, 1, 1, nr, cg, w))[:, 0, 0], SPACE, pair
        )
        for side, pair in zip(sides, pairs)
    ]
    local = [index, near_core(own), *map(near_core, x_halos)]

    flat_w = weight.transpose(0, 1, 2, 4, 3).reshape(27, cg, ch)
    span = rows // chips + 2
    (more,) = call(pack_more_kernel, [sds((chips, 27 + 2 * span, cg, ch), BF)], [index, flat_w, *map(near_core, g_halos)], smem=1)
    mine = swap_all(more, CHIPS)
    other = lax.ppermute(mine, "core", swap)

    keep, send = call(
        wgrad_kernel,
        [pltpu.VMEM((chips, 27, cg, ch), F32)] * 2,
        local,
        scratch=[pltpu.VMEM((nz + 2, 9 * ch, nh * w), BF), pltpu.VMEM((nz, ch, nh * w), BF)],
        smem=1,
        flops=2 * 27 * ch * ch * nz * nh * w,
    )
    got = lax.ppermute(send, "core", swap)
    pair = keep + got
    pieces = swap_all(pair, CHIPS).reshape(chips, 27, cg, ch)
    (padded,) = call(chips_add_kernel, [pltpu.VMEM((ns, cg, ch), F32)], [near_core(pieces)])

    near = call(
        conv_kernel,
        [pltpu.VMEM((4, 2, nz, nh, cg, w), F32)] * 4,
        local + [mine, other],
        scratch=[pltpu.VMEM((2, nz + 2, 9 * ch, nh * w), BF)] + [pltpu.VMEM((3, ch, 9 * ch), BF)] * 2,
        smem=1,
        flops=4 * 27 * ch * ch * nz * nh * w,
    )
    near = (
        near[0],
        lax.ppermute(near[1], "core", swap),
        lax.ppermute(near[2], "zl", swap),
        lax.ppermute(near[3], ("zl", "core"), [(i, 3 - i) for i in range(4)]),
    )
    shares = swap_all(padded, SPACE)
    _, near = lax.optimization_barrier((padded, near))
    (tap,) = call(functools.partial(space_add_kernel, norm=norm), [pltpu.VMEM((ns, cg, ch), F32)], [near_core(shares)])
    taps = swap_all(tap, SPACE)
    blocks = {j: jnp.stack([part[j] for part in near]) for j in range(4)}
    for j in (2, 1, 3):
        blocks[j] = lax.ppermute(blocks[j], "x", [(i, i ^ j) for i in range(4)])
    output, grad_in = call(
        place_kernel, [sds((nz, rows, cg, w), F32)] * 2, [index] + [near_core(blocks[j]) for j in range(4)], smem=1
    )
    weight_grad = taps[:27].reshape(3, 3, 3, cg, ch).transpose(0, 1, 2, 4, 3)
    return output, grad_in, weight_grad


def solution(mesh):
    fine = Mesh(mesh.devices.reshape(8, 4, 2, 4, 2), SPACE + FILT)
    return jax.shard_map(
        step,
        mesh=fine,
        in_specs=(
            P(SPACE, None, FILT, None),
            P(None, None, None, None, FILT),
            P(SPACE, None, FILT, None),
        ),
        out_specs=(
            P(SPACE, None, FILT, None),
            P(SPACE, None, FILT, None),
            P(None, None, None, None, FILT),
        ),
        check_vma=False,
    )
```

```python
import functools
import math

import jax
import jax.numpy as jnp
from jax import lax
from jax.experimental import pallas as pl
from jax.experimental.pallas import tpu as pltpu
from jax.sharding import Mesh
from jax.sharding import PartitionSpec as P


SPACE = ("y", "zh")
FILT = ("zl", "x", "core")
CHIPS = ("zl", "x")
BF, F32 = jnp.bfloat16, jnp.float32


def vmem_specs(n):
    return [pl.BlockSpec(memory_space=pltpu.VMEM)] * n


def call(kernel, outs, ins, scratch=(), smem=0, flops=0, copied=0):
    specs = [pl.BlockSpec(memory_space=pltpu.SMEM)] * smem + vmem_specs(len(ins) - smem)
    moved = sum(a.size * a.dtype.itemsize for a in ins) + sum(math.prod(o.shape) * 4 for o in outs)
    one = len(outs) == 1
    out_specs = vmem_specs(len(outs))
    if copied:
        out_specs = [pl.BlockSpec(memory_space=pl.ANY)]
        scratch = [pltpu.VMEM(outs[0].shape, outs[0].dtype), pltpu.SemaphoreType.DMA((copied,))]
    result = pl.pallas_call(
        kernel,
        out_shape=outs[0] if one else tuple(outs),
        in_specs=specs,
        out_specs=out_specs[0] if one else tuple(out_specs),
        scratch_shapes=list(scratch),
        cost_estimate=pl.CostEstimate(flops=flops, transcendentals=0, bytes_accessed=moved),
    )(*ins)
    return (result,) if one else result


def near_core(array):
    return pltpu.with_memory_space_constraint(array, pltpu.VMEM)


def place_of(index):
    return (index >> 3) & 1, (index >> 1) & 3, index & 1


def odd_slab(index):
    return (index >> 4) & 1 == 1


def pack_kernel(x_ref, g_ref, out_ref, o_ref, sems):
    n, _, nz, nr = o_ref.shape[:4]
    rows = x_ref.shape[1]
    zero = jnp.zeros(x_ref.shape[2:], x_ref.dtype)
    copies = [pltpu.make_async_copy(o_ref.at[d], out_ref.at[d], sems.at[d]) for d in range(n)]
    for d in range(n):
        for k, ref in enumerate((x_ref, g_ref)):
            for z in range(nz):
                for r in range(nr):
                    h = d * (nr - 2) + r - 1
                    o_ref[d, k, z, r] = ref[z, h] if 0 <= h < rows else zero
        copies[d].start()
    for copy in copies:
        copy.wait()


def halo_pick(index):
    odd = odd_slab(index)

    def pick(side, even, odd_side):
        even, odd_side = even.astype(F32), odd_side.astype(F32)
        return jnp.where(odd == (side == 0), even, odd_side).astype(BF)

    return pick


def pack_more_kernel(p_ref, w_ref, even_ref, odd_ref, out_ref, o_ref, sems):
    chips, total = o_ref.shape[:2]
    taps = w_ref.shape[0]
    rows = even_ref.shape[0]
    nr = (total - taps) // 2
    pick = halo_pick(p_ref[0])
    zero = jnp.zeros(w_ref.shape[1:], w_ref.dtype)
    copies = [pltpu.make_async_copy(o_ref.at[q], out_ref.at[q], sems.at[q]) for q in range(chips)]
    for q in range(chips):
        for t in range(taps):
            o_ref[q, t] = w_ref[t]
        for p in range(2):
            for r in range(nr):
                h = q * (nr - 2) + r - 1
                o_ref[q, taps + p * nr + r] = pick(p, even_ref[h], odd_ref[h]) if 0 <= h < rows else zero
        copies[q].start()
    for copy in copies:
        copy.wait()


def shifted(value):
    lane = lax.broadcasted_iota(jnp.int32, value.shape, 1)
    w = value.shape[1]
    left = jnp.where(lane == 0, 0.0, pltpu.roll(value, 1, 1))
    right = jnp.where(lane == w - 1, 0.0, pltpu.roll(value, w - 1, 1))
    return left.astype(BF), value.astype(BF), right.astype(BF)


def stack(parts):
    return jnp.concatenate([p.astype(F32) for p in parts], 0)


def by_core(first, mine, other):
    parts = []
    for m, o in zip(mine, other):
        m, o = m.astype(F32), o.astype(F32)
        parts += [jnp.where(first, m, o), jnp.where(first, o, m)]
    return jnp.concatenate(parts, 0)


def build(planes, sizes, s_ref):
    nr, ch, w = sizes
    for p, plane in enumerate(planes):
        for r in range(nr):
            for c, v in enumerate(shifted(plane(r))):
                for h in range(nr - 2):
                    b = r - h
                    if 0 <= b < 3:
                        s_ref[p, pl.ds((3 * b + c) * ch, ch), pl.ds(h * w, w)] = v


def own_plane(own_ref, k, z):
    return lambda r: stack([own_ref[d, k, z, r] for d in range(own_ref.shape[0])])


def halo_plane(index, side, even_ref, odd_ref):
    take_even = odd_slab(index) == (side == 0)

    def rows(r):
        n = even_ref.shape[0]
        return jnp.where(take_even, stack([even_ref[d, r] for d in range(n)]), stack([odd_ref[d, r] for d in range(n)]))

    return rows


def x_planes(index, own_ref, even_ref, odd_ref):
    inner = [own_plane(own_ref, 0, z) for z in range(own_ref.shape[2])]
    return [halo_plane(index, 0, even_ref, odd_ref)] + inner + [halo_plane(index, 1, even_ref, odd_ref)]


def wgrad_kernel(p_ref, own_ref, even_ref, odd_ref, keep_ref, send_ref, s_ref, t_ref):
    n, _, nz, nr, cg, w = own_ref.shape
    nh, ch = nr - 2, n * cg
    build(x_planes(p_ref[0], own_ref, even_ref, odd_ref), (nr, ch, w), s_ref)
    for z in range(nz):
        for h in range(nh):
            t_ref[z, :, pl.ds(h * w, w)] = own_plane(own_ref, 1, z)(h + 1).astype(BF)
    first = place_of(p_ref[0])[2] == 0
    for a in range(3):
        for b in range(3):
            total = None
            for z in range(nz):
                part = lax.dot_general(
                    t_ref[z],
                    s_ref[z + a, pl.ds(3 * b * ch, 3 * ch), :],
                    (((1,), (1,)), ((), ())),
                    preferred_element_type=F32,
                )
                total = part if total is None else total + part
            for c in range(3):
                tap = 9 * a + 3 * b + c
                for q in range(n // 2):
                    left, right = [
                        total[d * cg : (d + 1) * cg, c * ch : (c + 1) * ch] for d in (2 * q, 2 * q + 1)
                    ]
                    keep_ref[q, tap] = jnp.where(first, left, right)
                    send_ref[q, tap] = jnp.where(first, right, left)


def conv_kernel(
    p_ref, own_ref, even_ref, odd_ref, mine_ref, other_ref, out0, out1, out2, out3, s_ref, wt_ref, wf_ref
):
    n, _, nz, nr, cg, w = own_ref.shape
    nh, ch = nr - 2, n * cg
    chips, total = mine_ref.shape[:2]
    taps = 27
    span = (total - taps) // 2
    zl, x, core = place_of(p_ref[0])
    first = core == 0
    outs = (out0, out1, out2, out3)

    def targets(dx):
        return [[zl_to * 8 + dx * 2 + core_to for core_to in range(2)] for zl_to in range(2)]

    for t in range(taps):
        a, bc = t // 9, t % 9
        block = by_core(first, [mine_ref[q, t] for q in range(chips)], [other_ref[q, t] for q in range(chips)])
        wt_ref[a, :, pl.ds(bc * ch, ch)] = block.astype(BF)
        wf_ref[2 - a, :, pl.ds((8 - bc) * ch, ch)] = block.T.astype(BF)

    def g_halo(p):
        def rows(r):
            i = taps + p * span + r + core * nh
            return by_core(first, [mine_ref[q, i] for q in range(chips)], [other_ref[q, i] for q in range(chips)])

        return rows

    g_planes = [g_halo(0)] + [own_plane(own_ref, 1, z) for z in range(nz)] + [g_halo(1)]
    build(x_planes(p_ref[0], own_ref, even_ref, odd_ref), (nr, ch, w), s_ref.at[0])
    build(g_planes, (nr, ch, w), s_ref.at[1])
    for k, w_ref in enumerate((wt_ref, wf_ref)):
        for z in range(nz):
            total = None
            for a in range(3):
                part = jnp.dot(w_ref[a], s_ref[k, z + a], preferred_element_type=F32)
                total = part if total is None else total + part
            for dx in range(4):
                for h in range(nh):
                    tiles = [[total[d * cg : (d + 1) * cg, h * w : (h + 1) * w] for d in pair] for pair in targets(dx)]
                    tiles = [
                        [jnp.where(core == 0, t[0], t[1]), jnp.where(core == 0, t[1], t[0])] for t in tiles
                    ]
                    for j in range(2):
                        low = jnp.where(zl == 0, tiles[0][j], tiles[1][j])
                        high = jnp.where(zl == 0, tiles[1][j], tiles[0][j])
                        outs[j][dx ^ x, k, z, h] = low
                        outs[2 + j][dx ^ x, k, z, h] = high


def chips_add_kernel(pieces_ref, o_ref):
    taps = pieces_ref.shape[1]
    for t in range(o_ref.shape[0]):
        if t < taps:
            total = pieces_ref[0, t]
            for q in range(1, pieces_ref.shape[0]):
                total = total + pieces_ref[q, t]
        else:
            total = jnp.zeros(o_ref.shape[1:], F32)
        o_ref[t] = total


def space_add_kernel(shares_ref, o_ref, *, norm):
    total = shares_ref[0]
    for j in range(1, shares_ref.shape[0]):
        total = total + shares_ref[j]
    total = total * norm
    for j in range(o_ref.shape[0]):
        o_ref[j] = total


def place_kernel(p_ref, *refs):
    parts, outs = refs[:-2], refs[-2:]
    zl, x, core = place_of(p_ref[0])
    for dx, ref in enumerate(parts):
        for j in range(ref.shape[0]):
            source = ((zl ^ (j >> 1)) * 4 + (x ^ dx)) * 2 + (core ^ (j & 1))
            for k, o_ref in enumerate(outs):
                for z in range(ref.shape[2]):
                    for h in range(ref.shape[3]):
                        o_ref[z, source * ref.shape[3] + h] = ref[j, k, z, h]


def swap_all(array, axes):
    return lax.all_to_all(array, axes, 0, 0, tiled=True)


def step(activations, weight, grad_out):
    nz, rows, cg, w = activations.shape
    n = lax.axis_size(FILT)
    chips = lax.axis_size(CHIPS)
    ns = lax.axis_size(SPACE)
    ch = n * cg
    nr = rows // n + 2
    nh = nr - 2
    norm = float(nz * ns * rows * w) ** (-0.5)
    index = lax.axis_index(SPACE + FILT).astype(jnp.int32).reshape(1)
    parity = lax.axis_index(SPACE).astype(jnp.int32) & 1
    sides = [(nz - 1) * (1 - parity), (nz - 1) * parity]
    pairs = [[(i, i + 1) for i in range(first, ns - 1, 2)] for first in (0, 1)]
    pairs = [p + [(j, i) for i, j in p] for p in pairs]
    swap = [(0, 1), (1, 0)]
    sds = jax.ShapeDtypeStruct
    g_halos = [
        lax.ppermute(lax.dynamic_slice(grad_out, (side, 0, 0, 0), (1, rows, cg, w))[0], SPACE, pair)
        for side, pair in zip(sides, pairs)
    ]
    (packed,) = call(pack_kernel, [sds((n, 2, nz, nr, cg, w), BF)], [activations, grad_out], copied=n)
    own = swap_all(packed, FILT)
    x_halos = [
        lax.ppermute(
            lax.dynamic_slice(own, (0, 0, side, 0, 0, 0), (n, 1, 1, nr, cg, w))[:, 0, 0], SPACE, pair
        )
        for side, pair in zip(sides, pairs)
    ]
    local = [index, near_core(own), *map(near_core, x_halos)]

    flat_w = weight.transpose(0, 1, 2, 4, 3).reshape(27, cg, ch)
    span = rows // chips + 2
    (more,) = call(
        pack_more_kernel,
        [sds((chips, 27 + 2 * span, cg, ch), BF)],
        [index, flat_w, *map(near_core, g_halos)],
        smem=1,
        copied=chips,
    )
    mine = swap_all(more, CHIPS)
    other = lax.ppermute(mine, "core", swap)

    keep, send = call(
        wgrad_kernel,
        [pltpu.VMEM((chips, 27, cg, ch), F32)] * 2,
        local,
        scratch=[pltpu.VMEM((nz + 2, 9 * ch, nh * w), BF), pltpu.VMEM((nz, ch, nh * w), BF)],
        smem=1,
        flops=2 * 27 * ch * ch * nz * nh * w,
    )
    got = lax.ppermute(send, "core", swap)
    pair = keep + got
    pieces = swap_all(pair, CHIPS).reshape(chips, 27, cg, ch)
    (padded,) = call(chips_add_kernel, [pltpu.VMEM((ns, cg, ch), F32)], [near_core(pieces)])

    near = call(
        conv_kernel,
        [pltpu.VMEM((4, 2, nz, nh, cg, w), F32)] * 4,
        local + [mine, other],
        scratch=[pltpu.VMEM((2, nz + 2, 9 * ch, nh * w), BF)] + [pltpu.VMEM((3, ch, 9 * ch), BF)] * 2,
        smem=1,
        flops=4 * 27 * ch * ch * nz * nh * w,
    )
    both = lax.ppermute(near[3], ("zl", "core"), [(i, 3 - i) for i in range(4)])
    across = lax.ppermute(near[2], "zl", swap)

    shares = swap_all(padded, SPACE)
    beside = lax.ppermute(near[1], "core", swap)
    _, near = lax.optimization_barrier((padded, (near[0], beside, across, both)))
    (tap,) = call(functools.partial(space_add_kernel, norm=norm), [pltpu.VMEM((ns, cg, ch), F32)], [near_core(shares)])
    taps = swap_all(tap, SPACE)
    blocks = {j: jnp.stack([part[j] for part in near]) for j in range(4)}
    for j in (2, 1, 3):
        blocks[j] = lax.ppermute(blocks[j], "x", [(i, i ^ j) for i in range(4)])
    output, grad_in = call(
        place_kernel, [sds((nz, rows, cg, w), F32)] * 2, [index] + [near_core(blocks[j]) for j in range(4)], smem=1
    )
    weight_grad = taps[:27].reshape(3, 3, 3, cg, ch).transpose(0, 1, 2, 4, 3)
    return output, grad_in, weight_grad


def solution(mesh):
    fine = Mesh(mesh.devices.reshape(8, 4, 2, 4, 2), SPACE + FILT)
    return jax.shard_map(
        step,
        mesh=fine,
        in_specs=(
            P(SPACE, None, FILT, None),
            P(None, None, None, None, FILT),
            P(SPACE, None, FILT, None),
        ),
        out_specs=(
            P(SPACE, None, FILT, None),
            P(SPACE, None, FILT, None),
            P(None, None, None, None, FILT),
        ),
        check_vma=False,
    )
```
